32 devices in a mesh: expert: 8 (over z, core), hid: 4 (over y, x).
Axes of the slice: x: 2, y: 2, z: 4, core: 2. Of those that a mesh axis runs over, the one named last changes fastest.
Arguments:
- tokens: bfloat16 [64, 3584], P('expert', 'hid'), may hold values from -6 to 6
- cotangent: bfloat16 [64, 3584], P('expert', 'hid'), may hold values from -6 to 6
- gate_prob: float32 [64, 8], P('expert'), may hold values from 0.1 to 1
- routes: int32 [64, 8], P('expert'), may hold values from 0 to 7, as said below
- slots: int32 [64, 8], P('expert'), may hold values from 0 to 8, as said below
- drop_seed: int32 [1], replicated, may hold values from 0 to 16777215
- layer_id: int32 [1], replicated, may hold values from 0 to 63
- w_gate: bfloat16 [8, 2560, 3584], P('expert', 'hid'), may hold values from -0.09375 to 0.09375
- w_up: bfloat16 [8, 2560, 3584], P('expert', 'hid'), may hold values from -0.09375 to 0.09375
- w_down: bfloat16 [8, 2560, 3584], P('expert', 'hid'), may hold values from -0.125 to 0.125
Outputs:
- grad_tokens: bfloat16 [64, 3584], P('expert', 'hid')
- grad_gate: bfloat16 [8, 2560, 3584], P('expert', 'hid')
- grad_up: bfloat16 [8, 2560, 3584], P('expert', 'hid')
- grad_down: bfloat16 [8, 2560, 3584], P('expert', 'hid')
The draws below stay inside these ranges and needn't reach their ends.
Inputs may be any that keep to these rules, and one draw needn't show every extreme that they name: `routes`: each row names 8 different experts; one expert, drawn from the seed, is named by every token. Within one token group, the choices of each expert, taken in a priority order drawn from the seed, get slots 0, 1, 2 and so on, each slot at most once; those past 8 - 1 get the drop marker 8.
All inputs are finite; a program needn't handle non-finite values.
Results may differ from the reference program's by a relative error of at most 0.012.
Values may be sent and summed in bfloat16 or wider, within the bound.
No kernel may reach another device: no remote copies, remote signals or barrier semaphores. Data moves between devices by JAX's collectives and lax.ppermute only.
A program may use at most 64 MiB of HBM per device.

```python
import jax
import jax.numpy as jnp
from jax import lax

D = 3584
FF = 2560
TOP = 8
CAP_SRC = 8
EXPERTS = 8
CAPACITY = 64
TOK_GRP = 8
TOKENS = 64
N_HID = 4


def routing_pair(key):
    base = jax.random.fold_in(key, 7)
    first, second, third, fourth = jax.random.split(base, 4)
    favoured = jax.random.randint(first, (), 0, EXPERTS)
    expert_ids = jnp.arange(EXPERTS, dtype=jnp.int32)
    leaning = jax.random.randint(second, (EXPERTS,), 0, 3 * 4096)
    leaning = jnp.where(expert_ids == favoured, 64 * 4096, leaning)
    raw_score = jax.random.randint(third, (TOKENS, EXPERTS), 0, 16 * 4096)
    scores = (raw_score + leaning[None, :]) * EXPERTS + expert_ids[None, :]
    unused, chosen = lax.top_k(scores, TOP)
    chosen = chosen.astype(jnp.int32)
    groups = TOKENS // TOK_GRP
    members = TOK_GRP * TOP
    grouped = chosen.reshape(groups, members)
    order_ids = jnp.arange(members, dtype=jnp.int32)
    priority = jax.random.randint(fourth, (groups, members), 0, 1048576) * members + order_ids[None, :]
    same_expert = grouped[:, :, None] == grouped[:, None, :]
    earlier = priority[:, None, :] < priority[:, :, None]
    position = jnp.sum((same_expert & earlier).astype(jnp.int32), axis=2).reshape(TOKENS, TOP)
    position = jnp.minimum(position, CAP_SRC).astype(jnp.int32)
    return (chosen, position)


def draw_routes(key, part):
    chosen, position = routing_pair(key)
    return chosen


def draw_slots(key, part):
    chosen, position = routing_pair(key)
    return position


def shard_levels(stream_key, shape, cuts, low, largest):
    def one(dim, shards_of):
        heights = jax.random.uniform(jax.random.fold_in(jax.random.fold_in(stream_key, 6), dim), (shards_of,), jnp.float32, low / len(cuts), largest / len(cuts))
        return jnp.repeat(jnp.exp(heights), shape[dim] // shards_of).reshape((-1,) + (1,) * (len(shape) - dim - 1))

    loudness = one(*cuts[0])
    for cut in cuts[1:]:
        loudness = loudness * one(*cut)
    return loudness


def bell_draw(stream_key, extent, width, most, cuts=(), held_as=jnp.bfloat16):
    drawn = jax.random.normal(stream_key, extent, jnp.float32) * width
    if len(cuts) > 0:
        drawn = shard_levels(stream_key, extent, cuts, -0.22, 0.18) * drawn
    return jnp.clip(drawn, min=-most, max=most).astype(held_as)


def setup_inputs(seed: int = 0) -> dict:
    arg_keys = jax.random.split(jax.random.key(seed), 11)
    tokens = bell_draw(arg_keys[0], (TOKENS, D), 1.0, 6.0, ((0, 8), (1, 4)))
    cotangent = bell_draw(arg_keys[1], (TOKENS, D), 1.0, 6.0, ((0, 8), (1, 4)))
    gate_prob = jnp.clip(0.1 + 0.9 * jax.random.uniform(arg_keys[2], (TOKENS, TOP), jnp.float32) ** shard_levels(arg_keys[2], (TOKENS, TOP), ((0, 8),), -0.2, 0.2), 0.1, 1.0)
    routes = draw_routes(jax.random.fold_in(arg_keys[10], 71), 0)
    slots = draw_slots(jax.random.fold_in(arg_keys[10], 71), 0)
    drop_seed = jax.random.randint(arg_keys[5], (1,), 0, 16777216).astype(jnp.int32)
    layer_id = jax.random.randint(arg_keys[6], (1,), 0, 64).astype(jnp.int32)
    w_gate = bell_draw(arg_keys[7], (EXPERTS, FF, D), D ** -0.5, 0.09375, ((0, 8), (1, 4)))
    w_up = bell_draw(arg_keys[8], (EXPERTS, FF, D), D ** -0.5, 0.09375, ((0, 8), (1, 4)))
    w_down = bell_draw(arg_keys[9], (EXPERTS, FF, D), FF ** -0.5, 0.125, ((0, 8), (1, 4)))
    return {"tokens": tokens, "cotangent": cotangent, "gate_prob": gate_prob, "routes": routes, "slots": slots, "drop_seed": drop_seed, "layer_id": layer_id, "w_gate": w_gate, "w_up": w_up, "w_down": w_down}


KEEP_FACTOR = 1024.0 / 922.0


def logical_shift(values, amount):
    return jnp.right_shift(values, amount) & ((1 << (32 - amount)) - 1)


def keep_mask(counter, seed_value, layer_value):
    mixed = counter * (-1640531535) + seed_value * 40503 + layer_value * 97
    mixed = mixed ^ logical_shift(mixed, 15)
    mixed = mixed * (-2048144789)
    mixed = mixed ^ logical_shift(mixed, 13)
    mixed = mixed * (-1028477387)
    mixed = mixed ^ logical_shift(mixed, 16)
    levels = logical_shift(mixed, 8) & 1023
    return jnp.where(levels >= 102, KEEP_FACTOR, 0.0).astype(jnp.float32)


def reference(tokens, cotangent, gate_prob, routes, slots, drop_seed, layer_id, w_gate, w_up, w_down):
    group_of = (jnp.arange(TOKENS, dtype=jnp.int32) // TOK_GRP)[:, None]
    target = jnp.where(slots < CAP_SRC, routes * CAPACITY + group_of * CAP_SRC + slots, EXPERTS * CAPACITY).reshape(-1)
    spread_x = jnp.repeat(tokens, TOP, axis=0)
    spread_dy = (gate_prob[:, :, None] * cotangent.astype(jnp.float32)[:, None, :]).astype(jnp.bfloat16).reshape(TOKENS * TOP, D)
    all_x = jnp.zeros((EXPERTS * CAPACITY + 1, D), jnp.bfloat16).at[target].set(spread_x)
    all_dy = jnp.zeros((EXPERTS * CAPACITY + 1, D), jnp.bfloat16).at[target].set(spread_dy)
    rows_x = all_x[:-1].reshape(EXPERTS, CAPACITY, D)
    rows_dy = all_dy[:-1].reshape(EXPERTS, CAPACITY, D)
    seed_value = drop_seed[0]
    layer_value = layer_id[0]
    block = FF // N_HID
    contract_last = (((1,), (1,)), ((), ()))
    contract_first = (((0,), (0,)), ((), ()))

    def one_expert(inputs):
        exp_x, exp_dy, gate_w, up_w, down_w, expert_id = inputs
        gate_pre = lax.dot_general(exp_x, gate_w, contract_last, preferred_element_type=jnp.float32)
        up_pre = lax.dot_general(exp_x, up_w, contract_last, preferred_element_type=jnp.float32)
        row_ids = jnp.arange(CAPACITY, dtype=jnp.int32)[:, None]
        unit_ids = jnp.arange(FF, dtype=jnp.int32)[None, :]
        counter = (expert_id * CAPACITY + row_ids) * FF + unit_ids
        keep_mul = keep_mask(counter, seed_value, layer_value)
        logistic = jax.nn.sigmoid(gate_pre)
        swish = gate_pre * logistic
        hidden = (swish * up_pre * keep_mul).astype(jnp.bfloat16)
        grad_hidden = lax.dot_general(exp_dy, down_w, contract_last, preferred_element_type=jnp.float32) * keep_mul
        grad_upre = (grad_hidden * swish).astype(jnp.bfloat16)
        grad_gpre = (grad_hidden * up_pre * logistic * (1.0 + gate_pre * (1.0 - logistic))).astype(jnp.bfloat16)
        grad_down = lax.dot_general(hidden, exp_dy, contract_first, preferred_element_type=jnp.float32).astype(jnp.bfloat16)
        grad_gate = lax.dot_general(grad_gpre, exp_x, contract_first, preferred_element_type=jnp.float32).astype(jnp.bfloat16)
        grad_up = lax.dot_general(grad_upre, exp_x, contract_first, preferred_element_type=jnp.float32).astype(jnp.bfloat16)
        gpre_blocks = grad_gpre.astype(jnp.float32).reshape(CAPACITY, N_HID, block)
        upre_blocks = grad_upre.astype(jnp.float32).reshape(CAPACITY, N_HID, block)
        gate_blocks = gate_w.astype(jnp.float32).reshape(N_HID, block, D)
        up_blocks = up_w.astype(jnp.float32).reshape(N_HID, block, D)
        pieces = jnp.einsum('rhf,hfd->hrd', gpre_blocks, gate_blocks) + jnp.einsum('rhf,hfd->hrd', upre_blocks, up_blocks)
        rounded = lax.optimization_barrier(pieces.astype(jnp.bfloat16))
        grad_rows = jnp.sum(rounded.astype(jnp.float32), axis=0).astype(jnp.bfloat16)
        return grad_gate, grad_up, grad_down, grad_rows

    expert_ids = jnp.arange(EXPERTS, dtype=jnp.int32)
    grad_gate, grad_up, grad_down, grad_rows = lax.map(one_expert, (rows_x, rows_dy, w_gate, w_up, w_down, expert_ids))
    flat_rows = jnp.concatenate([grad_rows.reshape(EXPERTS * CAPACITY, D), jnp.zeros((1, D), jnp.bfloat16)], axis=0)
    picked = flat_rows[target].reshape(TOKENS, TOP, D).astype(jnp.float32)
    grad_tokens = jnp.sum(picked, axis=1).astype(jnp.bfloat16)
    return grad_tokens, grad_gate, grad_up, grad_down
```

```python
import jax
import jax.numpy as jnp
from jax import lax
from jax.experimental import pallas as pl
from jax.experimental.pallas import tpu as pltpu
from jax.sharding import PartitionSpec as P

FF = 2560
CAP_SRC = 8


KEEP_FACTOR = 1024.0 / 922.0


def logical_shift(values, amount):
    return jnp.right_shift(values, amount) & (1 << 32 - amount) - 1


def keep_mask(counter, seed_value, layer_value):
    mixed = counter * -1640531535 + seed_value * 40503 + layer_value * 97
    mixed = mixed ^ logical_shift(mixed, 15)
    mixed = mixed * -2048144789
    mixed = mixed ^ logical_shift(mixed, 13)
    mixed = mixed * -1028477387
    mixed = mixed ^ logical_shift(mixed, 16)
    levels = logical_shift(mixed, 8) & 1023
    return jnp.where(levels >= 102, KEEP_FACTOR, 0.0).astype(jnp.float32)


def contract_rows(left, right):
    return lax.dot_general(
        left, right, (((0,), (0,)), ((), ())), preferred_element_type=jnp.float32
    )


def contract_cols(left, right):
    return lax.dot_general(
        left, right, (((1,), (1,)), ((), ())), preferred_element_type=jnp.float32
    )


def general_device(
    tokens, cotangent, gate_prob, routes, slots, drop_seed, layer_id, w_gate, w_up, w_down
):
    experts = lax.axis_size("expert")
    part_width = tokens.shape[1]
    capacity = experts * CAP_SRC
    local_units = w_gate.shape[1]
    target = jnp.where(slots < CAP_SRC, routes * CAP_SRC + slots, -1)
    slot_ids = jnp.arange(experts * CAP_SRC, dtype=jnp.int32)
    matches = target[None, :, :] == slot_ids[:, None, None]
    placed = jnp.any(matches, axis=2).astype(jnp.bfloat16)
    slot_gate = jnp.sum(jnp.where(matches, gate_prob[None, :, :], 0.0), axis=(1, 2))
    sent_x = jnp.dot(placed, tokens, preferred_element_type=jnp.float32).astype(jnp.bfloat16)
    plain_dy = jnp.dot(placed, cotangent, preferred_element_type=jnp.float32)
    sent_dy = (slot_gate[:, None] * plain_dy).astype(jnp.bfloat16)
    send_shape = (experts, CAP_SRC * part_width)
    recv_x, recv_dy = (
        lax.all_to_all(
            sent_x.reshape(send_shape), "expert", split_axis=0, concat_axis=0, tiled=True
        ),
        lax.all_to_all(
            sent_dy.reshape(send_shape), "expert", split_axis=0, concat_axis=0, tiled=True
        ),
    )
    rows_x, rows_dy = (
        lax.all_gather(recv_x.reshape(capacity, part_width), "hid", axis=1, tiled=True),
        lax.all_gather(recv_dy.reshape(capacity, part_width), "hid", axis=1, tiled=True),
    )
    gate_w = w_gate[0]
    up_w = w_up[0]
    down_w = w_down[0]
    gate_pre = contract_cols(rows_x, gate_w)
    up_pre = contract_cols(rows_x, up_w)
    expert_id = lax.axis_index("expert")
    unit_ids = lax.axis_index("hid") * local_units + jnp.arange(local_units, dtype=jnp.int32)
    row_ids = jnp.arange(capacity, dtype=jnp.int32)
    counter = (expert_id * capacity + row_ids[:, None]) * FF + unit_ids[None, :]
    keep_mul = keep_mask(counter, drop_seed[0], layer_id[0])
    logistic = jax.nn.sigmoid(gate_pre)
    swish = gate_pre * logistic
    hidden = (swish * up_pre * keep_mul).astype(jnp.bfloat16)
    grad_hidden = contract_cols(rows_dy, down_w) * keep_mul
    grad_upre = (grad_hidden * swish).astype(jnp.bfloat16)
    grad_gpre = (grad_hidden * up_pre * logistic * (1.0 + gate_pre * (1.0 - logistic))).astype(
        jnp.bfloat16
    )
    grad_down = contract_rows(hidden, rows_dy).astype(jnp.bfloat16)
    grad_gate = contract_rows(grad_gpre, rows_x).astype(jnp.bfloat16)
    grad_up = contract_rows(grad_upre, rows_x).astype(jnp.bfloat16)
    partial_sum = jnp.dot(grad_gpre, gate_w, preferred_element_type=jnp.float32) + jnp.dot(
        grad_upre, up_w, preferred_element_type=jnp.float32
    )
    summed = lax.psum(partial_sum.astype(jnp.bfloat16), "hid").astype(jnp.float32)
    own_cols = lax.dynamic_slice_in_dim(summed, lax.axis_index("hid") * part_width, part_width, 1)
    back_rows = lax.all_to_all(
        own_cols.astype(jnp.bfloat16).reshape(send_shape),
        "expert",
        split_axis=0,
        concat_axis=0,
        tiled=True,
    )
    grad_tokens = contract_rows(placed, back_rows.reshape(experts * CAP_SRC, part_width)).astype(
        jnp.bfloat16
    )
    return (grad_tokens, grad_gate[None], grad_up[None], grad_down[None])


BF16 = jnp.bfloat16
F32 = jnp.float32
AXES = ("expert", "hid")


def relative_order(size):
    order = [0]
    bits = [1 << b for b in range(1, size.bit_length() - 1)][::-1] + [1]
    for bit in bits:
        order = order + [o ^ bit for o in order]
    return order


def swap(value, distance, size):
    return lax.ppermute(value, AXES, [(i, i ^ distance) for i in range(size)])


def logical(values, amount):
    return lax.shift_right_logical(values, jnp.full(values.shape, amount, jnp.int32))


def contract_last(left, right):
    return lax.dot_general(
        left, right, (((1,), (1,)), ((), ())), preferred_element_type=F32
    )


def hidden_kernel(
    place_ref, x_ref, c_ref, gate_ref, base_ref, wg_hbm, wu_hbm, wd_hbm,
    piece_ref, dy_ref, hid_t_ref, gpre_t_ref, upre_t_ref,
    wg, wu, wd, sems,
):
    parts, rows, width = x_ref.shape
    units = wg.shape[0]
    me = place_ref[0]

    def copies(j):
        cols = pl.ds(pl.multiple_of((me ^ j) * width, 128), width)
        return [
            pltpu.make_async_copy(src.at[:, cols], dst.at[:, cols], sems.at[j, k])
            for k, (src, dst) in enumerate(((wg_hbm, wg), (wu_hbm, wu), (wd_hbm, wd)))
        ]

    for j in range(parts):
        for copy in copies(j):
            copy.start()
    gate = gate_ref[...]
    unit_ids = me * units + lax.broadcasted_iota(jnp.int32, (rows, units), 1)
    mixed = base_ref[...] + unit_ids * -1640531535
    mixed = mixed ^ logical(mixed, 15)
    mixed = mixed * -2048144789
    mixed = mixed ^ logical(mixed, 13)
    mixed = mixed * -1028477387
    mixed = mixed ^ logical(mixed, 16)
    levels = logical(mixed, 8) & 1023
    keep_mul = jnp.where(levels >= 102, KEEP_FACTOR, 0.0).astype(F32)
    gate_pre = up_pre = grad_hidden = None
    for j in range(parts):
        cols = pl.ds(pl.multiple_of((me ^ j) * width, 128), width)
        x = x_ref[j]
        dy = (gate * c_ref[j].astype(F32)).astype(BF16)
        dy_ref[j] = dy
        for copy in copies(j):
            copy.wait()
        terms = (
            contract_last(x, wg[:, cols]),
            contract_last(x, wu[:, cols]),
            contract_last(dy, wd[:, cols]),
        )
        if j == 0:
            gate_pre, up_pre, grad_hidden = terms
        else:
            gate_pre, up_pre, grad_hidden = (
                gate_pre + terms[0], up_pre + terms[1], grad_hidden + terms[2]
            )
    grad_hidden = grad_hidden * keep_mul
    logistic = jax.nn.sigmoid(gate_pre)
    swish = gate_pre * logistic
    hidden = swish * up_pre * keep_mul
    upre = grad_hidden * swish
    gpre = grad_hidden * up_pre * logistic * (1.0 + gate_pre * (1.0 - logistic))
    hid_t_ref[...] = hidden.T.astype(BF16)
    gpre_t_ref[...] = gpre.T.astype(BF16)
    upre_t_ref[...] = upre.T.astype(BF16)
    gpre = gpre.astype(BF16)
    upre = upre.astype(BF16)
    for j in range(parts):
        cols = pl.ds(pl.multiple_of((me ^ j) * width, 128), width)
        piece_ref[j] = (
            jnp.dot(gpre, wg[:, cols], preferred_element_type=F32)
            + jnp.dot(upre, wu[:, cols], preferred_element_type=F32)
        ).astype(BF16)


def weight_kernel(place_ref, left_ref, right_ref, out_ref):
    out_ref[...] = jnp.dot(
        left_ref[...], right_ref[0], preferred_element_type=F32
    ).astype(BF16)


def weight_grad(place, left, right):
    parts, rows, width = right.shape
    units = left.shape[0]
    return pl.pallas_call(
        weight_kernel,
        grid_spec=pltpu.PrefetchScalarGridSpec(
            num_scalar_prefetch=1,
            grid=(parts,),
            in_specs=[
                pl.BlockSpec((units, rows), lambda j, place: (0, 0)),
                pl.BlockSpec((1, rows, width), lambda j, place: (j, 0, 0)),
            ],
            out_specs=pl.BlockSpec((units, width), lambda j, place: (0, place[0] ^ j)),
        ),
        out_shape=jax.ShapeDtypeStruct((units, parts * width), BF16),
        cost_estimate=pl.CostEstimate(
            flops=2 * units * rows * parts * width,
            bytes_accessed=2 * units * parts * width,
            transcendentals=0,
        ),
    )(place, left, right)


def token_device(
    tokens, cotangent, gate_prob, routes, slots, drop_seed, layer_id, w_gate, w_up, w_down
):
    experts = lax.axis_size("expert")
    parts = lax.axis_size("hid")
    size = experts * parts
    group, width = tokens.shape
    units = w_gate.shape[1]
    rows = experts * group
    expert_id = lax.axis_index("expert")
    hid_id = lax.axis_index("hid")
    top = gate_prob.shape[1]
    high = gate_prob.astype(BF16)
    rest = gate_prob - high.astype(F32)
    middle = rest.astype(BF16)
    low = (rest - middle.astype(F32)).astype(BF16)
    notes = jnp.concatenate(
        [routes.astype(BF16), slots.astype(BF16), high, middle, low,
         jnp.zeros((group, 128 - 5 * top), BF16)], axis=1)
    data = jnp.concatenate(
        [jnp.concatenate([tokens, notes], axis=1),
         jnp.concatenate([cotangent, jnp.zeros((group, 128), BF16)], axis=1)], axis=0)[None]
    distance = experts // 2
    while distance > 1:
        data = jnp.concatenate([data, swap(data, distance * parts, size)], axis=0)
        distance //= 2
    notes = data[:, :group, width:]
    data = data[:, :, :width]
    notes = jnp.concatenate([notes, swap(notes, parts, size)], axis=0).reshape(rows, 128)
    data = jnp.stack([data] + [swap(data, j, size) for j in range(1, parts)], axis=0)
    data = jnp.concatenate([data, swap(data, parts, size)], axis=1)
    x = data[:, :, :group].reshape(parts, rows, width)
    c = data[:, :, group:].reshape(parts, rows, width)
    order = jnp.array(relative_order(experts), jnp.int32)
    group_ids = jnp.repeat(order ^ expert_id, group)[:, None]
    notes = notes.astype(F32)
    route, slot, high, middle, low = (notes[:, i * top:(i + 1) * top] for i in range(5))
    chosen = (route == expert_id.astype(F32)) & (slot < CAP_SRC)
    gate = jnp.sum(jnp.where(chosen, high + middle + low, 0.0), axis=1, keepdims=True)
    slot = jnp.sum(jnp.where(chosen, slot, 0.0), axis=1, keepdims=True).astype(jnp.int32)
    row_ids = expert_id * (experts * CAP_SRC) + group_ids * CAP_SRC + slot
    base = row_ids * FF * -1640531535 + drop_seed[0] * 40503 + layer_id[0] * 97
    place = hid_id.astype(jnp.int32)[None]
    any_spec = pl.BlockSpec(memory_space=pl.ANY)
    vmem_spec = pl.BlockSpec(memory_space=pltpu.VMEM)
    turned = jax.ShapeDtypeStruct((units, rows), BF16)
    spread = jax.ShapeDtypeStruct((parts, rows, width), BF16)
    piece, dy, hid_t, gpre_t, upre_t = pl.pallas_call(
        hidden_kernel,
        in_specs=[pl.BlockSpec(memory_space=pltpu.SMEM)] + [vmem_spec] * 4 + [any_spec] * 3,
        out_specs=[vmem_spec] * 5,
        out_shape=[spread, spread, turned, turned, turned],
        scratch_shapes=[pltpu.VMEM((units, parts * width), BF16)] * 3
        + [pltpu.SemaphoreType.DMA((parts, 3))],
        compiler_params=pltpu.CompilerParams(vmem_limit_bytes=32 * 1024 * 1024),
        cost_estimate=pl.CostEstimate(
            flops=10 * units * rows * parts * width,
            bytes_accessed=6 * units * parts * width,
            transcendentals=rows * units,
        ),
    )(place, x, c, gate, base, w_gate[0], w_up[0], w_down[0])
    part = piece.reshape(parts, experts, group, width)
    half = experts // 2

    def add(kept, came):
        return (kept.astype(F32) + came.astype(F32)).astype(BF16)

    part = add(part[:, :half], swap(part[:, half:], parts, size))
    distance = parts // 2
    while distance:
        count = part.shape[0] // 2
        part = add(part[:count], swap(part[count:], distance, size))
        distance //= 2
    part = part[0]
    distance = 2
    while distance < experts:
        count = part.shape[0] // 2
        part = add(part[:count], swap(part[count:], distance * parts, size))
        distance *= 2
    grad_tokens = part[0]
    grad_down = weight_grad(place, hid_t, dy)
    grad_gate = weight_grad(place, gpre_t, x)
    grad_up = weight_grad(place, upre_t, x)
    return (grad_tokens, grad_gate[None], grad_up[None], grad_down[None])


def power_of_two(number):
    return number & (number - 1) == 0


def on_device(*args):
    tokens, gate_prob = args[0], args[2]
    experts = lax.axis_size("expert")
    parts = lax.axis_size("hid")
    small = tokens.shape[0] <= CAP_SRC and 5 * gate_prob.shape[1] <= 128
    even = power_of_two(experts) and power_of_two(parts) and experts > 1
    tiled = tokens.shape[1] % 128 == 0 and args[7].shape[1] % 128 == 0
    if small and even and tiled and tokens.shape[0] % 8 == 0 and experts <= 256:
        return token_device(*args)
    return general_device(*args)


def solution(mesh):
    in_specs = (
        P("expert", "hid"),
        P("expert", "hid"),
        P("expert", None),
        P("expert", None),
        P("expert", None),
        P(),
        P(),
        P("expert", "hid", None),
        P("expert", "hid", None),
        P("expert", "hid", None),
    )
    out_specs = (
        P("expert", "hid"),
        P("expert", "hid", None),
        P("expert", "hid", None),
        P("expert", "hid", None),
    )
    return jax.shard_map(
        on_device, mesh=mesh, in_specs=in_specs, out_specs=out_specs, check_vma=False
    )
```

```python
import jax
import jax.numpy as jnp
from jax import lax
from jax.experimental import pallas as pl
from jax.experimental.pallas import tpu as pltpu
from jax.sharding import PartitionSpec as P

FF = 2560
CAP_SRC = 8


KEEP_FACTOR = 1024.0 / 922.0


def logical_shift(values, amount):
    return jnp.right_shift(values, amount) & (1 << 32 - amount) - 1


def keep_mask(counter, seed_value, layer_value):
    mixed = counter * -1640531535 + seed_value * 40503 + layer_value * 97
    mixed = mixed ^ logical_shift(mixed, 15)
    mixed = mixed * -2048144789
    mixed = mixed ^ logical_shift(mixed, 13)
    mixed = mixed * -1028477387
    mixed = mixed ^ logical_shift(mixed, 16)
    levels = logical_shift(mixed, 8) & 1023
    return jnp.where(levels >= 102, KEEP_FACTOR, 0.0).astype(jnp.float32)


def contract_rows(left, right):
    return lax.dot_general(
        left, right, (((0,), (0,)), ((), ())), preferred_element_type=jnp.float32
    )


def contract_cols(left, right):
    return lax.dot_general(
        left, right, (((1,), (1,)), ((), ())), preferred_element_type=jnp.float32
    )


def general_device(
    tokens, cotangent, gate_prob, routes, slots, drop_seed, layer_id, w_gate, w_up, w_down
):
    experts = lax.axis_size("expert")
    part_width = tokens.shape[1]
    capacity = experts * CAP_SRC
    local_units = w_gate.shape[1]
    target = jnp.where(slots < CAP_SRC, routes * CAP_SRC + slots, -1)
    slot_ids = jnp.arange(experts * CAP_SRC, dtype=jnp.int32)
    matches = target[None, :, :] == slot_ids[:, None, None]
    placed = jnp.any(matches, axis=2).astype(jnp.bfloat16)
    slot_gate = jnp.sum(jnp.where(matches, gate_prob[None, :, :], 0.0), axis=(1, 2))
    sent_x = jnp.dot(placed, tokens, preferred_element_type=jnp.float32).astype(jnp.bfloat16)
    plain_dy = jnp.dot(placed, cotangent, preferred_element_type=jnp.float32)
    sent_dy = (slot_gate[:, None] * plain_dy).astype(jnp.bfloat16)
    send_shape = (experts, CAP_SRC * part_width)
    recv_x, recv_dy = (
        lax.all_to_all(
            sent_x.reshape(send_shape), "expert", split_axis=0, concat_axis=0, tiled=True
        ),
        lax.all_to_all(
            sent_dy.reshape(send_shape), "expert", split_axis=0, concat_axis=0, tiled=True
        ),
    )
    rows_x, rows_dy = (
        lax.all_gather(recv_x.reshape(capacity, part_width), "hid", axis=1, tiled=True),
        lax.all_gather(recv_dy.reshape(capacity, part_width), "hid", axis=1, tiled=True),
    )
    gate_w = w_gate[0]
    up_w = w_up[0]
    down_w = w_down[0]
    gate_pre = contract_cols(rows_x, gate_w)
    up_pre = contract_cols(rows_x, up_w)
    expert_id = lax.axis_index("expert")
    unit_ids = lax.axis_index("hid") * local_units + jnp.arange(local_units, dtype=jnp.int32)
    row_ids = jnp.arange(capacity, dtype=jnp.int32)
    counter = (expert_id * capacity + row_ids[:, None]) * FF + unit_ids[None, :]
    keep_mul = keep_mask(counter, drop_seed[0], layer_id[0])
    logistic = jax.nn.sigmoid(gate_pre)
    swish = gate_pre * logistic
    hidden = (swish * up_pre * keep_mul).astype(jnp.bfloat16)
    grad_hidden = contract_cols(rows_dy, down_w) * keep_mul
    grad_upre = (grad_hidden * swish).astype(jnp.bfloat16)
    grad_gpre = (grad_hidden * up_pre * logistic * (1.0 + gate_pre * (1.0 - logistic))).astype(
        jnp.bfloat16
    )
    grad_down = contract_rows(hidden, rows_dy).astype(jnp.bfloat16)
    grad_gate = contract_rows(grad_gpre, rows_x).astype(jnp.bfloat16)
    grad_up = contract_rows(grad_upre, rows_x).astype(jnp.bfloat16)
    partial_sum = jnp.dot(grad_gpre, gate_w, preferred_element_type=jnp.float32) + jnp.dot(
        grad_upre, up_w, preferred_element_type=jnp.float32
    )
    summed = lax.psum(partial_sum.astype(jnp.bfloat16), "hid").astype(jnp.float32)
    own_cols = lax.dynamic_slice_in_dim(summed, lax.axis_index("hid") * part_width, part_width, 1)
    back_rows = lax.all_to_all(
        own_cols.astype(jnp.bfloat16).reshape(send_shape),
        "expert",
        split_axis=0,
        concat_axis=0,
        tiled=True,
    )
    grad_tokens = contract_rows(placed, back_rows.reshape(experts * CAP_SRC, part_width)).astype(
        jnp.bfloat16
    )
    return (grad_tokens, grad_gate[None], grad_up[None], grad_down[None])


BF16 = jnp.bfloat16
F32 = jnp.float32
I32 = jnp.int32
AXES = ("expert", "hid")
LANES = 128
HBM = pl.BlockSpec(memory_space=pltpu.HBM)
VMEM = pl.BlockSpec(memory_space=pltpu.VMEM)
SMEM = pl.BlockSpec(memory_space=pltpu.SMEM)


def shape(dims, dtype=BF16):
    return jax.ShapeDtypeStruct(dims, dtype)


def call(kernel, ins, outs, out_shape, scratch=(), flops=0, moved=0, vmem=8):
    return pl.pallas_call(
        kernel,
        in_specs=ins,
        out_specs=outs,
        out_shape=out_shape,
        scratch_shapes=list(scratch),
        compiler_params=pltpu.CompilerParams(vmem_limit_bytes=vmem * 1024 * 1024),
        cost_estimate=pl.CostEstimate(flops=flops, bytes_accessed=moved, transcendentals=0),
    )


def swap(value, distance, size):
    return lax.ppermute(value, AXES, [(i, i ^ distance) for i in range(size)])


def logical(values, amount):
    return lax.shift_right_logical(values, jnp.full(values.shape, amount, I32))


def contract_last(left, right):
    return lax.dot_general(
        left, right, (((1,), (1,)), ((), ())), preferred_element_type=F32
    )


def columns(me, part, parts, width):
    return pl.ds(pl.multiple_of(((me % parts) ^ part) * width, LANES), width)


def pack(tokens, cotangent, gate_prob, routes, slots):
    group, width = tokens.shape
    top = gate_prob.shape[1]

    def put(value, row, start):
        stop = width + LANES - start - value.shape[1]
        zero = jnp.zeros((), value.dtype)
        return lax.pad(value[None], zero, ((row, 1 - row, 0), (0, 0, 0), (start, stop, 0)))

    def rounded(value):
        return lax.reduce_precision(value, 8, 7)

    high, middle, low = (put(gate_prob, 0, width + i * top) for i in (2, 3, 4))
    rest = low - rounded(low)
    return (
        put(tokens, 0, 0).astype(F32)
        + put(cotangent, 1, 0).astype(F32)
        + put(routes, 0, width).astype(F32)
        + put(slots, 0, width + top).astype(F32)
        + rounded(high)
        + rounded(middle - rounded(middle))
        + (rest - rounded(rest))
    ).astype(BF16)


def load_kernel(count, *refs):
    sems = refs[-1]
    copies = [
        pltpu.make_async_copy(refs[i], refs[count + 1 + i], sems.at[i]) for i in range(count)
    ]
    for copy in copies:
        copy.start()
    for copy in copies:
        copy.wait()


def load(weights, after, vmem):
    count = len(weights)
    return call(
        lambda *refs: load_kernel(count, *refs), [HBM] * count + [VMEM], [VMEM] * count,
        [shape(w.shape) for w in weights], [pltpu.SemaphoreType.DMA((count,))],
        moved=2 * count * weights[0].size, vmem=vmem,
    )(*weights, after)


def plan_kernel(bits, parts, top, place_ref, seed_ref, layer_ref, own_ref, other_ref, *refs):
    gate_ref, base_ref = refs[-2:]
    notes = jnp.concatenate([own_ref[...], other_ref[...]], axis=0).astype(F32)
    rows = notes.shape[0]
    group = rows >> bits
    expert = place_ref[0] // parts
    lane = lax.broadcasted_iota(I32, (rows, LANES), 1)

    def field(i):
        return pltpu.roll(notes, LANES - i * top, 1) if i else notes

    slots = field(1)
    chosen = (
        (lane < top)
        & (field(0) == jnp.full((rows, LANES), expert, I32).astype(F32))
        & (slots < CAP_SRC)
    )
    gate = jnp.where(chosen, field(2) + field(3) + field(4), 0.0)
    gate_ref[...] = jnp.sum(gate, axis=1, keepdims=True)
    slot = jnp.sum(jnp.where(chosen, slots, 0.0), axis=1, keepdims=True).astype(I32)
    position = lax.broadcasted_iota(I32, (rows, 1), 0) // group
    offset = jnp.zeros((rows, 1), I32)
    for b in range(bits):
        offset = offset + (((position >> b) & 1) << (bits - 1 - b))
    row_ids = (expert << bits) * CAP_SRC + (offset ^ expert) * CAP_SRC + slot
    base_ref[...] = row_ids * FF * -1640531535 + seed_ref[0] * 40503 + layer_ref[0] * 97


def pre_kernel(part, first, *refs):
    place_ref, own_ref, other_ref, gate_ref, wg, wu, wd = refs[:7]
    x_ref, dy_ref, acc_ref = refs[-3:]
    width = own_ref.shape[2]
    cols = columns(place_ref[0], part, wg.shape[1] // width, width)
    x = jnp.concatenate([own_ref[0], other_ref[0]], axis=0)
    c = jnp.concatenate([own_ref[1], other_ref[1]], axis=0)
    dy = (gate_ref[...] * c.astype(F32)).astype(BF16)
    x_ref[...] = x
    dy_ref[...] = dy
    for i, (left, weight) in enumerate(((x, wg), (x, wu), (dy, wd))):
        term = contract_last(left, weight[:, cols])
        acc_ref[i] = term if first else refs[7][i] + term


def pieces(me, part_ids, g, u, wg, wu, keep_ref, send_ref):
    _, half, width = keep_ref.shape
    for i, part in enumerate(part_ids):
        cols = columns(me, part, wg.shape[1] // width, width)
        piece = (
            jnp.dot(g, wg[:, cols], preferred_element_type=F32)
            + jnp.dot(u, wu[:, cols], preferred_element_type=F32)
        ).astype(BF16)
        keep_ref[i] = piece[:half]
        send_ref[i] = piece[half:]


def hidden_kernel(
    part_ids, place_ref, base_ref, acc_ref, wg, wu,
    keep_ref, send_ref, g_ref, u_ref, hid_t_ref, g_t_ref, u_t_ref,
):
    me = place_ref[0]
    _, rows, units = acc_ref.shape
    width = keep_ref.shape[2]
    unit_ids = (me % (wg.shape[1] // width)) * units + lax.broadcasted_iota(I32, (rows, units), 1)
    mixed = base_ref[...] + unit_ids * -1640531535
    mixed = mixed ^ logical(mixed, 15)
    mixed = mixed * -2048144789
    mixed = mixed ^ logical(mixed, 13)
    mixed = mixed * -1028477387
    mixed = mixed ^ logical(mixed, 16)
    levels = logical(mixed, 8) & 1023
    keep_mul = jnp.where(levels >= 102, KEEP_FACTOR, 0.0).astype(F32)
    gate_pre = acc_ref[0]
    up_pre = acc_ref[1]
    grad_hidden = acc_ref[2] * keep_mul
    logistic = jax.nn.sigmoid(gate_pre)
    swish = gate_pre * logistic
    upre = grad_hidden * swish
    gpre = grad_hidden * up_pre * logistic * (1.0 + gate_pre * (1.0 - logistic))
    g = gpre.astype(BF16)
    u = upre.astype(BF16)
    g_ref[...] = g
    u_ref[...] = u
    pieces(me, part_ids, g, u, wg, wu, keep_ref, send_ref)
    hid_t_ref[...] = (swish * up_pre * keep_mul).T.astype(BF16)
    g_t_ref[...] = gpre.T.astype(BF16)
    u_t_ref[...] = upre.T.astype(BF16)


def piece_kernel(part_ids, place_ref, g_ref, u_ref, wg, wu, keep_ref, send_ref):
    pieces(place_ref[0], part_ids, g_ref[...], u_ref[...], wg, wu, keep_ref, send_ref)


def weight_kernel(place_ref, left_ref, *refs):
    rights, out_ref, held, sems = refs[:-3], refs[-3], refs[-2], refs[-1]
    width = rights[0].shape[1]
    copies = []
    for j, right in enumerate(rights):
        held[j] = jnp.dot(
            left_ref[...], right[...], preferred_element_type=F32
        ).astype(BF16)
        copies.append(
            pltpu.make_async_copy(
                held.at[j], out_ref.at[:, columns(place_ref[0], j, len(rights), width)], sems.at[j]
            )
        )
        copies[-1].start()
    for copy in copies:
        copy.wait()


def weight_grad(place, left, rights):
    parts = len(rights)
    rows, width = rights[0].shape
    units = left.shape[0]
    return call(
        weight_kernel, [SMEM, VMEM] + [VMEM] * parts, HBM, shape((units, parts * width)),
        [pltpu.VMEM((parts, units, width), BF16), pltpu.SemaphoreType.DMA((parts,))],
        flops=2 * units * rows * parts * width, moved=2 * units * parts * width, vmem=12,
    )(place, left, *rights)


def add(kept, came):
    return (kept.astype(F32) + came.astype(F32)).astype(BF16)


def token_device(
    tokens, cotangent, gate_prob, routes, slots, drop_seed, layer_id, w_gate, w_up, w_down
):
    experts = lax.axis_size("expert")
    parts = lax.axis_size("hid")
    size = experts * parts
    group, width = tokens.shape
    top = gate_prob.shape[1]
    units = w_gate.shape[1]
    rows = experts * group
    half = rows // 2
    bits = experts.bit_length() - 1
    place = lax.axis_index(AXES).astype(I32)[None]
    wg, wu, wd = w_gate[0], w_up[0], w_down[0]
    data = pack(tokens, cotangent, gate_prob, routes, slots)
    data, place = lax.optimization_barrier((data, place))
    distance = experts // 2
    loads, loaded = [([wg], 48), ([wu, wd], 40)], []
    while distance > 1:
        came = swap(data, distance * parts, size)
        if loads:
            held = load(loads[0][0], data, loads[0][1])
            came, *held = lax.optimization_barrier((came, *held))
            loads, loaded = loads[1:], loaded + held
        data = jnp.concatenate([data, came], axis=1)
        distance //= 2
    wg, wu, wd = loaded + [w for pair in loads for w in pair[0]]
    notes = data[0, :, width:]
    own = [data[:, :, :width]]
    own += [swap(own[0], j, size) for j in range(1, parts)]
    other_notes = swap(notes, parts, size)
    gate, base = call(
        lambda *refs: plan_kernel(bits, parts, top, *refs),
        [SMEM] * 3 + [VMEM] * 2, [VMEM] * 2,
        [shape((rows, 1), F32), shape((rows, 1), I32)],
    )(place, drop_seed, layer_id, notes, other_notes)
    xs, dys, acc = [None] * parts, [None] * parts, None
    order = [0] + list(range(1, parts))[::-1]
    order = order[:2] + order[2:][::-1]
    others = [swap(own[0], parts, size)] + [None] * (parts - 1)
    for n, j in enumerate(order):
        held = [] if acc is None else [acc]
        other = others[j]
        xs[j], dys[j], acc = call(
            lambda *refs, j=j, n=n: pre_kernel(j, n == 0, *refs),
            [SMEM] + [VMEM] * (6 + len(held)), [VMEM] * 3,
            [shape((rows, width)), shape((rows, width)), shape((3, rows, units), F32)],
            flops=6 * rows * units * width, moved=6 * units * width,
        )(place, own[j], other, gate, wg, wu, wd, *held)
        if n == 0:
            came = lax.optimization_barrier((acc, own[order[1]]))
            acc, own[order[1]] = came
            others[order[1]] = swap(own[order[1]], parts, size)
        if n + 2 < parts:
            i, k = order[n + 1], order[n + 2]
            others[k] = swap(own[k], parts, size)
            others[i], others[k] = others[i], others[k]
    high = list(range(parts // 2, parts))
    low = list(range(parts // 2))
    block = shape((parts // 2, half, width))
    turned = shape((units, rows))
    straight = shape((rows, units))
    flops = 4 * rows * units * width * (parts // 2)
    keep, send, g, u, hid_t, g_t, u_t = call(
        lambda *refs: hidden_kernel(high, *refs), [SMEM] + [VMEM] * 4, [VMEM] * 7,
        [block, block, straight, straight, turned, turned, turned],
        flops=flops, moved=2 * units * width * parts,
    )(place, base, acc, wg, wu)
    upper = add(keep, swap(send, parts, size))
    keep, send = call(
        lambda *refs: piece_kernel(low, *refs), [SMEM] + [VMEM] * 4, [VMEM] * 2,
        [block, block], flops=flops, moved=2 * units * width * parts,
    )(place, g, u, wg, wu)
    lower = add(keep, swap(send, parts, size))
    lefts, rights, grads = [hid_t, g_t, u_t], [dys, xs, xs], []

    def exchange(kept, sent, distance):
        if len(grads) == len(lefts):
            return add(kept, swap(sent, distance, size))
        i = len(grads)
        sent, left = lax.optimization_barrier((sent, lefts[i]))
        came = swap(sent, distance, size)
        grad = weight_grad(place, left, rights[i])
        came, grad = lax.optimization_barrier((came, grad))
        grads.append(grad)
        return add(kept, came)

    part = exchange(lower, upper, parts // 2)
    distance = parts // 4
    while distance:
        count = part.shape[0] // 2
        part = exchange(part[:count], part[count:], distance)
        distance //= 2
    part = part[0].reshape(experts // 2, group, width)
    distance = 2
    while distance < experts:
        count = part.shape[0] // 2
        part = exchange(part[:count], part[count:], distance * parts)
        distance *= 2
    for i in range(len(grads), len(lefts)):
        grads.append(weight_grad(place, lefts[i], rights[i]))
    grad_down, grad_gate, grad_up = grads
    return (part[0], grad_gate[None], grad_up[None], grad_down[None])


def power_of_two(number):
    return number & (number - 1) == 0


def on_device(*args):
    tokens, gate_prob, w_gate = args[0], args[2], args[7]
    experts = lax.axis_size("expert")
    parts = lax.axis_size("hid")
    few = tokens.shape[0] <= CAP_SRC and experts <= 256
    noted = 5 * gate_prob.shape[1] <= LANES
    even = power_of_two(experts) and power_of_two(parts) and experts > 1 and parts > 1
    tiled = (
        tokens.shape[0] % 8 == 0
        and tokens.shape[1] % LANES == 0
        and w_gate.shape[1] % LANES == 0
    )
    if few and noted and even and tiled:
        return token_device(*args)
    return general_device(*args)


def solution(mesh):
    in_specs = (
        P("expert", "hid"),
        P("expert", "hid"),
        P("expert", None),
        P("expert", None),
        P("expert", None),
        P(),
        P(),
        P("expert", "hid", None),
        P("expert", "hid", None),
        P("expert", "hid", None),
    )
    out_specs = (
        P("expert", "hid"),
        P("expert", "hid", None),
        P("expert", "hid", None),
        P("expert", "hid", None),
    )
    return jax.shard_map(
        on_device, mesh=mesh, in_specs=in_specs, out_specs=out_specs, check_vma=False
    )
```

```python
import jax
import jax.numpy as jnp
from jax import lax
from jax.experimental import pallas as pl
from jax.experimental.pallas import tpu as pltpu
from jax.sharding import PartitionSpec as P

FF = 2560
CAP_SRC = 8


KEEP_FACTOR = 1024.0 / 922.0


def logical_shift(values, amount):
    return jnp.right_shift(values, amount) & (1 << 32 - amount) - 1


def keep_mask(counter, seed_value, layer_value):
    mixed = counter * -1640531535 + seed_value * 40503 + layer_value * 97
    mixed = mixed ^ logical_shift(mixed, 15)
    mixed = mixed * -2048144789
    mixed = mixed ^ logical_shift(mixed, 13)
    mixed = mixed * -1028477387
    mixed = mixed ^ logical_shift(mixed, 16)
    levels = logical_shift(mixed, 8) & 1023
    return jnp.where(levels >= 102, KEEP_FACTOR, 0.0).astype(jnp.float32)


def contract_rows(left, right):
    return lax.dot_general(
        left, right, (((0,), (0,)), ((), ())), preferred_element_type=jnp.float32
    )


def contract_cols(left, right):
    return lax.dot_general(
        left, right, (((1,), (1,)), ((), ())), preferred_element_type=jnp.float32
    )


def general_device(
    tokens, cotangent, gate_prob, routes, slots, drop_seed, layer_id, w_gate, w_up, w_down
):
    experts = lax.axis_size("expert")
    part_width = tokens.shape[1]
    capacity = experts * CAP_SRC
    local_units = w_gate.shape[1]
    target = jnp.where(slots < CAP_SRC, routes * CAP_SRC + slots, -1)
    slot_ids = jnp.arange(experts * CAP_SRC, dtype=jnp.int32)
    matches = target[None, :, :] == slot_ids[:, None, None]
    placed = jnp.any(matches, axis=2).astype(jnp.bfloat16)
    slot_gate = jnp.sum(jnp.where(matches, gate_prob[None, :, :], 0.0), axis=(1, 2))
    sent_x = jnp.dot(placed, tokens, preferred_element_type=jnp.float32).astype(jnp.bfloat16)
    plain_dy = jnp.dot(placed, cotangent, preferred_element_type=jnp.float32)
    sent_dy = (slot_gate[:, None] * plain_dy).astype(jnp.bfloat16)
    send_shape = (experts, CAP_SRC * part_width)
    recv_x, recv_dy = (
        lax.all_to_all(
            sent_x.reshape(send_shape), "expert", split_axis=0, concat_axis=0, tiled=True
        ),
        lax.all_to_all(
            sent_dy.reshape(send_shape), "expert", split_axis=0, concat_axis=0, tiled=True
        ),
    )
    rows_x, rows_dy = (
        lax.all_gather(recv_x.reshape(capacity, part_width), "hid", axis=1, tiled=True),
        lax.all_gather(recv_dy.reshape(capacity, part_width), "hid", axis=1, tiled=True),
    )
    gate_w = w_gate[0]
    up_w = w_up[0]
    down_w = w_down[0]
    gate_pre = contract_cols(rows_x, gate_w)
    up_pre = contract_cols(rows_x, up_w)
    expert_id = lax.axis_index("expert")
    unit_ids = lax.axis_index("hid") * local_units + jnp.arange(local_units, dtype=jnp.int32)
    row_ids = jnp.arange(capacity, dtype=jnp.int32)
    counter = (expert_id * capacity + row_ids[:, None]) * FF + unit_ids[None, :]
    keep_mul = keep_mask(counter, drop_seed[0], layer_id[0])
    logistic = jax.nn.sigmoid(gate_pre)
    swish = gate_pre * logistic
    hidden = (swish * up_pre * keep_mul).astype(jnp.bfloat16)
    grad_hidden = contract_cols(rows_dy, down_w) * keep_mul
    grad_upre = (grad_hidden * swish).astype(jnp.bfloat16)
    grad_gpre = (grad_hidden * up_pre * logistic * (1.0 + gate_pre * (1.0 - logistic))).astype(
        jnp.bfloat16
    )
    grad_down = contract_rows(hidden, rows_dy).astype(jnp.bfloat16)
    grad_gate = contract_rows(grad_gpre, rows_x).astype(jnp.bfloat16)
    grad_up = contract_rows(grad_upre, rows_x).astype(jnp.bfloat16)
    partial_sum = jnp.dot(grad_gpre, gate_w, preferred_element_type=jnp.float32) + jnp.dot(
        grad_upre, up_w, preferred_element_type=jnp.float32
    )
    summed = lax.psum(partial_sum.astype(jnp.bfloat16), "hid").astype(jnp.float32)
    own_cols = lax.dynamic_slice_in_dim(summed, lax.axis_index("hid") * part_width, part_width, 1)
    back_rows = lax.all_to_all(
        own_cols.astype(jnp.bfloat16).reshape(send_shape),
        "expert",
        split_axis=0,
        concat_axis=0,
        tiled=True,
    )
    grad_tokens = contract_rows(placed, back_rows.reshape(experts * CAP_SRC, part_width)).astype(
        jnp.bfloat16
    )
    return (grad_tokens, grad_gate[None], grad_up[None], grad_down[None])


BF16 = jnp.bfloat16
F32 = jnp.float32
I32 = jnp.int32
AXES = ("expert", "hid")
LANES = 128
HBM = pl.BlockSpec(memory_space=pltpu.HBM)
VMEM = pl.BlockSpec(memory_space=pltpu.VMEM)
SMEM = pl.BlockSpec(memory_space=pltpu.SMEM)


def shape(dims, dtype=BF16):
    return jax.ShapeDtypeStruct(dims, dtype)


def call(kernel, ins, outs, out_shape, scratch=(), flops=0, moved=0, vmem=8):
    return pl.pallas_call(
        kernel,
        in_specs=ins,
        out_specs=outs,
        out_shape=out_shape,
        scratch_shapes=list(scratch),
        compiler_params=pltpu.CompilerParams(vmem_limit_bytes=vmem * 1024 * 1024),
        cost_estimate=pl.CostEstimate(flops=flops, bytes_accessed=moved, transcendentals=0),
    )


def swap(value, distance, size):
    return lax.ppermute(value, AXES, [(i, i ^ distance) for i in range(size)])


def logical(values, amount):
    return lax.shift_right_logical(values, jnp.full(values.shape, amount, I32))


def contract_last(left, right):
    return lax.dot_general(
        left, right, (((1,), (1,)), ((), ())), preferred_element_type=F32
    )


def columns(me, part, parts, width):
    return pl.ds(pl.multiple_of(((me % parts) ^ part) * width, LANES), width)


def pack(tokens, cotangent, gate_prob, routes, slots):
    group, width = tokens.shape
    top = gate_prob.shape[1]

    def put(value, row, start):
        stop = width + LANES - start - value.shape[1]
        zero = jnp.zeros((), value.dtype)
        return lax.pad(value[None], zero, ((row, 1 - row, 0), (0, 0, 0), (start, stop, 0)))

    def rounded(value):
        return lax.reduce_precision(value, 8, 7)

    high, middle, low = (put(gate_prob, 0, width + i * top) for i in (2, 3, 4))
    rest = low - rounded(low)
    return (
        put(tokens, 0, 0).astype(F32)
        + put(cotangent, 1, 0).astype(F32)
        + put(routes, 0, width).astype(F32)
        + put(slots, 0, width + top).astype(F32)
        + rounded(high)
        + rounded(middle - rounded(middle))
        + (rest - rounded(rest))
    ).astype(BF16)


def load_kernel(count, *refs):
    sems = refs[-1]
    copies = [
        pltpu.make_async_copy(refs[i], refs[count + 1 + i], sems.at[i]) for i in range(count)
    ]
    for copy in copies:
        copy.start()
    for copy in copies:
        copy.wait()


def load(weights, after, vmem):
    count = len(weights)
    return call(
        lambda *refs: load_kernel(count, *refs), [HBM] * count + [VMEM], [VMEM] * count,
        [shape(w.shape) for w in weights], [pltpu.SemaphoreType.DMA((count,))],
        moved=2 * count * weights[0].size, vmem=vmem,
    )(*weights, after)


def plan_kernel(bits, parts, top, place_ref, seed_ref, layer_ref, own_ref, other_ref, *refs):
    gate_ref, base_ref = refs[-2:]
    notes = jnp.concatenate([own_ref[...], other_ref[...]], axis=0).astype(F32)
    rows = notes.shape[0]
    group = rows >> bits
    expert = place_ref[0] // parts
    lane = lax.broadcasted_iota(I32, (rows, LANES), 1)

    def field(i):
        return pltpu.roll(notes, LANES - i * top, 1) if i else notes

    slots = field(1)
    chosen = (
        (lane < top)
        & (field(0) == jnp.full((rows, LANES), expert, I32).astype(F32))
        & (slots < CAP_SRC)
    )
    gate = jnp.where(chosen, field(2) + field(3) + field(4), 0.0)
    gate_ref[...] = jnp.sum(gate, axis=1, keepdims=True)
    slot = jnp.sum(jnp.where(chosen, slots, 0.0), axis=1, keepdims=True).astype(I32)
    position = lax.broadcasted_iota(I32, (rows, 1), 0) // group
    offset = jnp.zeros((rows, 1), I32)
    for b in range(bits):
        offset = offset + (((position >> b) & 1) << (bits - 1 - b))
    row_ids = (expert << bits) * CAP_SRC + (offset ^ expert) * CAP_SRC + slot
    base_ref[...] = row_ids * FF * -1640531535 + seed_ref[0] * 40503 + layer_ref[0] * 97


def pre_kernel(part, first, *refs):
    place_ref, own_ref, other_ref, gate_ref, wg, wu, wd = refs[:7]
    x_ref, dy_ref, acc_ref = refs[-3:]
    width = own_ref.shape[2]
    cols = columns(place_ref[0], part, wg.shape[1] // width, width)
    x = jnp.concatenate([own_ref[0], other_ref[0]], axis=0)
    c = jnp.concatenate([own_ref[1], other_ref[1]], axis=0)
    dy = (gate_ref[...] * c.astype(F32)).astype(BF16)
    x_ref[...] = x
    dy_ref[...] = dy
    for i, (left, weight) in enumerate(((x, wg), (x, wu), (dy, wd))):
        term = contract_last(left, weight[:, cols])
        acc_ref[i] = term if first else refs[7][i] + term


def pieces(me, part_ids, g, u, wg, wu, keep_ref, send_ref):
    _, half, width = keep_ref.shape
    for i, part in enumerate(part_ids):
        cols = columns(me, part, wg.shape[1] // width, width)
        piece = (
            jnp.dot(g, wg[:, cols], preferred_element_type=F32)
            + jnp.dot(u, wu[:, cols], preferred_element_type=F32)
        ).astype(BF16)
        keep_ref[i] = piece[:half]
        send_ref[i] = piece[half:]


def hidden_kernel(
    part_ids, place_ref, base_ref, acc_ref, wg, wu,
    keep_ref, send_ref, g_ref, u_ref, hid_t_ref, g_t_ref, u_t_ref,
):
    me = place_ref[0]
    _, rows, units = acc_ref.shape
    width = keep_ref.shape[2]
    unit_ids = (me % (wg.shape[1] // width)) * units + lax.broadcasted_iota(I32, (rows, units), 1)
    mixed = base_ref[...] + unit_ids * -1640531535
    mixed = mixed ^ logical(mixed, 15)
    mixed = mixed * -2048144789
    mixed = mixed ^ logical(mixed, 13)
    mixed = mixed * -1028477387
    mixed = mixed ^ logical(mixed, 16)
    levels = logical(mixed, 8) & 1023
    keep_mul = jnp.where(levels >= 102, KEEP_FACTOR, 0.0).astype(F32)
    gate_pre = acc_ref[0]
    up_pre = acc_ref[1]
    grad_hidden = acc_ref[2] * keep_mul
    logistic = jax.nn.sigmoid(gate_pre)
    swish = gate_pre * logistic
    upre = grad_hidden * swish
    gpre = grad_hidden * up_pre * logistic * (1.0 + gate_pre * (1.0 - logistic))
    g = gpre.astype(BF16)
    u = upre.astype(BF16)
    g_ref[...] = g
    u_ref[...] = u
    pieces(me, part_ids, g, u, wg, wu, keep_ref, send_ref)
    hid_t_ref[...] = (swish * up_pre * keep_mul).T.astype(BF16)
    g_t_ref[...] = gpre.T.astype(BF16)
    u_t_ref[...] = upre.T.astype(BF16)


def piece_kernel(part_ids, place_ref, g_ref, u_ref, wg, wu, keep_ref, send_ref):
    pieces(place_ref[0], part_ids, g_ref[...], u_ref[...], wg, wu, keep_ref, send_ref)


def weight_kernel(jobs, parts, cuts, place_ref, *refs):
    outs, held, sems = refs[-len(jobs) - 2:-2], refs[-2], refs[-1]
    units, width = held.shape[1:]
    copies, n, at = [], 0, 0
    for out, ids in zip(outs, jobs):
        left = refs[at]
        for k, j in enumerate(ids):
            cols = columns(place_ref[0], j, parts, width)
            step = units // (cuts if n == 0 else 1)
            for r in range(0, units, step):
                rows = slice(r, r + step)
                held[n, rows] = jnp.dot(
                    left[rows], refs[at + 1 + k][...], preferred_element_type=F32
                ).astype(BF16)
                copies.append(
                    pltpu.make_async_copy(
                        held.at[n, rows], out.at[rows, cols], sems.at[len(copies)]
                    )
                )
                copies[-1].start()
            n += 1
        at += 1 + len(ids)
    for copy in copies:
        copy.wait()


def weight_grads(place, jobs):
    parts = len(jobs[0][1])
    rows, width = jobs[0][1][0].shape
    units = jobs[0][0].shape[0]
    cuts = 4 if units % 64 == 0 else 1
    ids = [job[2] for job in jobs]
    count = sum(len(i) for i in ids)
    flat = [x for left, right, i, _ in jobs for x in [left] + [right[j] for j in i]]
    begun = [job[3] for job in jobs if job[3] is not None]
    aliases, at = {}, 1 + len(flat)
    for n, job in enumerate(jobs):
        if job[3] is not None:
            aliases[at] = n
            at += 1
    return pl.pallas_call(
        lambda *refs: weight_kernel(ids, parts, cuts, *refs),
        in_specs=[SMEM] + [VMEM] * len(flat) + [HBM] * len(begun),
        out_specs=[HBM] * len(jobs),
        out_shape=[shape((units, parts * width))] * len(jobs),
        scratch_shapes=[
            pltpu.VMEM((count, units, width), BF16), pltpu.SemaphoreType.DMA((count + cuts - 1,))
        ],
        input_output_aliases=aliases,
        compiler_params=pltpu.CompilerParams(vmem_limit_bytes=20 * 1024 * 1024),
        cost_estimate=pl.CostEstimate(
            flops=2 * count * units * rows * width,
            bytes_accessed=2 * count * units * width,
            transcendentals=0,
        ),
    )(place, *flat, *begun)


def add(kept, *came):
    total = kept.astype(F32)
    for block in came:
        total = total + block.astype(F32)
    return total.astype(BF16)


def token_device(
    tokens, cotangent, gate_prob, routes, slots, drop_seed, layer_id, w_gate, w_up, w_down
):
    experts = lax.axis_size("expert")
    parts = lax.axis_size("hid")
    size = experts * parts
    group, width = tokens.shape
    top = gate_prob.shape[1]
    units = w_gate.shape[1]
    rows = experts * group
    half = rows // 2
    bits = experts.bit_length() - 1
    place = lax.axis_index(AXES).astype(I32)[None]
    wg, wu, wd = w_gate[0], w_up[0], w_down[0]
    data = pack(tokens, cotangent, gate_prob, routes, slots)
    data, place = lax.optimization_barrier((data, place))
    distance = experts // 2
    loads, loaded = [([wg], 48), ([wu, wd], 40)], []
    while distance > 1:
        came = swap(data, distance * parts, size)
        if loads:
            held = load(loads[0][0], data, loads[0][1])
            came, *held = lax.optimization_barrier((came, *held))
            loads, loaded = loads[1:], loaded + held
        data = jnp.concatenate([data, came], axis=1)
        distance //= 2
    wg, wu, wd = loaded + [w for pair in loads for w in pair[0]]
    notes = data[0, :, width:]
    own = [data[:, :, :width]]
    own += [swap(own[0], j, size) for j in range(1, parts)]
    other_notes = swap(notes, parts, size)
    gate, base = call(
        lambda *refs: plan_kernel(bits, parts, top, *refs),
        [SMEM] * 3 + [VMEM] * 2, [VMEM] * 2,
        [shape((rows, 1), F32), shape((rows, 1), I32)],
    )(place, drop_seed, layer_id, notes, other_notes)
    xs, dys, acc = [None] * parts, [None] * parts, None
    order = [0] + list(range(1, parts))[::-1]
    order = order[:2] + order[2:][::-1]
    others = [swap(own[0], parts, size)] + [None] * (parts - 1)
    for n, j in enumerate(order):
        held = [] if acc is None else [acc]
        other = others[j]
        xs[j], dys[j], acc = call(
            lambda *refs, j=j, n=n: pre_kernel(j, n == 0, *refs),
            [SMEM] + [VMEM] * (6 + len(held)), [VMEM] * 3,
            [shape((rows, width)), shape((rows, width)), shape((3, rows, units), F32)],
            flops=6 * rows * units * width, moved=6 * units * width,
        )(place, own[j], other, gate, wg, wu, wd, *held)
        if n == 0:
            came = lax.optimization_barrier((acc, own[order[1]]))
            acc, own[order[1]] = came
            others[order[1]] = swap(own[order[1]], parts, size)
        if n + 2 < parts:
            i, k = order[n + 1], order[n + 2]
            others[k] = swap(own[k], parts, size)
            others[i], others[k] = others[i], others[k]
    high = [parts - 1]
    low = list(range(parts - 1))
    block, blocks = (shape((len(ids), half, width)) for ids in (high, low))
    turned = shape((units, rows))
    straight = shape((rows, units))
    flops = 4 * rows * units * width * (parts // 2)
    keep, send, g, u, hid_t, g_t, u_t = call(
        lambda *refs: hidden_kernel(high, *refs), [SMEM] + [VMEM] * 4, [VMEM] * 7,
        [block, block, straight, straight, turned, turned, turned],
        flops=flops, moved=2 * units * width * parts,
    )(place, base, acc, wg, wu)
    upper_keep, upper_came = keep, swap(send, parts, size)
    keep, send = call(
        lambda *refs: piece_kernel(low, *refs), [SMEM] + [VMEM] * 4, [VMEM] * 2,
        [blocks, blocks], flops=flops, moved=2 * units * width * parts,
    )(place, g, u, wg, wu)
    upper_came, keep, send = lax.optimization_barrier((upper_came, keep, send))
    upper = add(upper_keep, upper_came)
    lower = add(keep, swap(send, parts, size))
    every, front, back = list(range(parts)), list(range(parts // 2)), list(range(parts // 2, parts))

    def rounds(kept, sends, after, jobs):
        came = [swap(block, distance, size) for block, distance in sends]
        made = []
        if jobs:
            lefts = lax.optimization_barrier((tuple(job[0] for job in jobs), after))[0]
            made = weight_grads(place, [(left, *job[1:]) for left, job in zip(lefts, jobs)])
            *came, made = lax.optimization_barrier((*came, made))
        return add(kept, *came), made

    sends = [(upper[i], part) for i, part in enumerate(high)][::-1]
    sends += [(lower[i], part) for i, part in enumerate(low)][:0:-1]
    waiting, _ = lax.optimization_barrier((tuple(block for block, _ in sends[1:]), lower))
    sends[1:] = [(block, send[1]) for block, send in zip(waiting, sends[1:])]
    part, (grad_down, grad_gate) = rounds(
        lower[0], sends, lower, [(hid_t, dys, every, None), (g_t, xs, front, None)]
    )
    part = part.reshape(experts // 2, group, width)
    distance, grad_up = experts // 2, None
    jobs = [(g_t, xs, back, grad_gate)]
    while distance > 1:
        kept, away = part[0::2], part[1::2]
        part, made = rounds(kept, [(away, distance * parts)], away, jobs)
        if distance == experts // 2:
            (grad_gate,), jobs = made, [(u_t, xs, every, None)]
        elif jobs:
            (grad_up,), jobs = made, []
        distance //= 2
    if experts == 2:
        (grad_gate,) = weight_grads(place, jobs)
    if grad_up is None:
        (grad_up,) = weight_grads(place, [(u_t, xs, every, None)])
    return (part[0], grad_gate[None], grad_up[None], grad_down[None])


def power_of_two(number):
    return number & (number - 1) == 0


def on_device(*args):
    tokens, gate_prob, w_gate = args[0], args[2], args[7]
    experts = lax.axis_size("expert")
    parts = lax.axis_size("hid")
    few = tokens.shape[0] <= CAP_SRC and experts <= 256
    noted = 5 * gate_prob.shape[1] <= LANES
    even = power_of_two(experts) and power_of_two(parts) and experts > 1 and parts > 1
    tiled = (
        tokens.shape[0] % 8 == 0
        and tokens.shape[1] % LANES == 0
        and w_gate.shape[1] % LANES == 0
    )
    if few and noted and even and tiled:
        return token_device(*args)
    return general_device(*args)


def solution(mesh):
    in_specs = (
        P("expert", "hid"),
        P("expert", "hid"),
        P("expert", None),
        P("expert", None),
        P("expert", None),
        P(),
        P(),
        P("expert", "hid", None),
        P("expert", "hid", None),
        P("expert", "hid", None),
    )
    out_specs = (
        P("expert", "hid"),
        P("expert", "hid", None),
        P("expert", "hid", None),
        P("expert", "hid", None),
    )
    return jax.shard_map(
        on_device, mesh=mesh, in_specs=in_specs, out_specs=out_specs, check_vma=False
    )
```

```python
import jax
import jax.numpy as jnp
from jax import lax
from jax.experimental import pallas as pl
from jax.experimental.pallas import tpu as pltpu
from jax.sharding import PartitionSpec as P

FF = 2560
CAP_SRC = 8


KEEP_FACTOR = 1024.0 / 922.0


def logical_shift(values, amount):
    return jnp.right_shift(values, amount) & (1 << 32 - amount) - 1


def keep_mask(counter, seed_value, layer_value):
    mixed = counter * -1640531535 + seed_value * 40503 + layer_value * 97
    mixed = mixed ^ logical_shift(mixed, 15)
    mixed = mixed * -2048144789
    mixed = mixed ^ logical_shift(mixed, 13)
    mixed = mixed * -1028477387
    mixed = mixed ^ logical_shift(mixed, 16)
    levels = logical_shift(mixed, 8) & 1023
    return jnp.where(levels >= 102, KEEP_FACTOR, 0.0).astype(jnp.float32)


def contract_rows(left, right):
    return lax.dot_general(
        left, right, (((0,), (0,)), ((), ())), preferred_element_type=jnp.float32
    )


def contract_cols(left, right):
    return lax.dot_general(
        left, right, (((1,), (1,)), ((), ())), preferred_element_type=jnp.float32
    )


def general_device(
    tokens, cotangent, gate_prob, routes, slots, drop_seed, layer_id, w_gate, w_up, w_down
):
    experts = lax.axis_size("expert")
    part_width = tokens.shape[1]
    capacity = experts * CAP_SRC
    local_units = w_gate.shape[1]
    target = jnp.where(slots < CAP_SRC, routes * CAP_SRC + slots, -1)
    slot_ids = jnp.arange(experts * CAP_SRC, dtype=jnp.int32)
    matches = target[None, :, :] == slot_ids[:, None, None]
    placed = jnp.any(matches, axis=2).astype(jnp.bfloat16)
    slot_gate = jnp.sum(jnp.where(matches, gate_prob[None, :, :], 0.0), axis=(1, 2))
    sent_x = jnp.dot(placed, tokens, preferred_element_type=jnp.float32).astype(jnp.bfloat16)
    plain_dy = jnp.dot(placed, cotangent, preferred_element_type=jnp.float32)
    sent_dy = (slot_gate[:, None] * plain_dy).astype(jnp.bfloat16)
    send_shape = (experts, CAP_SRC * part_width)
    recv_x, recv_dy = (
        lax.all_to_all(
            sent_x.reshape(send_shape), "expert", split_axis=0, concat_axis=0, tiled=True
        ),
        lax.all_to_all(
            sent_dy.reshape(send_shape), "expert", split_axis=0, concat_axis=0, tiled=True
        ),
    )
    rows_x, rows_dy = (
        lax.all_gather(recv_x.reshape(capacity, part_width), "hid", axis=1, tiled=True),
        lax.all_gather(recv_dy.reshape(capacity, part_width), "hid", axis=1, tiled=True),
    )
    gate_w = w_gate[0]
    up_w = w_up[0]
    down_w = w_down[0]
    gate_pre = contract_cols(rows_x, gate_w)
    up_pre = contract_cols(rows_x, up_w)
    expert_id = lax.axis_index("expert")
    unit_ids = lax.axis_index("hid") * local_units + jnp.arange(local_units, dtype=jnp.int32)
    row_ids = jnp.arange(capacity, dtype=jnp.int32)
    counter = (expert_id * capacity + row_ids[:, None]) * FF + unit_ids[None, :]
    keep_mul = keep_mask(counter, drop_seed[0], layer_id[0])
    logistic = jax.nn.sigmoid(gate_pre)
    swish = gate_pre * logistic
    hidden = (swish * up_pre * keep_mul).astype(jnp.bfloat16)
    grad_hidden = contract_cols(rows_dy, down_w) * keep_mul
    grad_upre = (grad_hidden * swish).astype(jnp.bfloat16)
    grad_gpre = (grad_hidden * up_pre * logistic * (1.0 + gate_pre * (1.0 - logistic))).astype(
        jnp.bfloat16
    )
    grad_down = contract_rows(hidden, rows_dy).astype(jnp.bfloat16)
    grad_gate = contract_rows(grad_gpre, rows_x).astype(jnp.bfloat16)
    grad_up = contract_rows(grad_upre, rows_x).astype(jnp.bfloat16)
    partial_sum = jnp.dot(grad_gpre, gate_w, preferred_element_type=jnp.float32) + jnp.dot(
        grad_upre, up_w, preferred_element_type=jnp.float32
    )
    summed = lax.psum(partial_sum.astype(jnp.bfloat16), "hid").astype(jnp.float32)
    own_cols = lax.dynamic_slice_in_dim(summed, lax.axis_index("hid") * part_width, part_width, 1)
    back_rows = lax.all_to_all(
        own_cols.astype(jnp.bfloat16).reshape(send_shape),
        "expert",
        split_axis=0,
        concat_axis=0,
        tiled=True,
    )
    grad_tokens = contract_rows(placed, back_rows.reshape(experts * CAP_SRC, part_width)).astype(
        jnp.bfloat16
    )
    return (grad_tokens, grad_gate[None], grad_up[None], grad_down[None])


BF16 = jnp.bfloat16
F32 = jnp.float32
I32 = jnp.int32
AXES = ("expert", "hid")
LANES = 128
HBM = pl.BlockSpec(memory_space=pltpu.HBM)
VMEM = pl.BlockSpec(memory_space=pltpu.VMEM)
SMEM = pl.BlockSpec(memory_space=pltpu.SMEM)


def shape(dims, dtype=BF16):
    return jax.ShapeDtypeStruct(dims, dtype)


def call(kernel, ins, outs, out_shape, scratch=(), flops=0, moved=0, vmem=8):
    return pl.pallas_call(
        kernel,
        in_specs=ins,
        out_specs=outs,
        out_shape=out_shape,
        scratch_shapes=list(scratch),
        compiler_params=pltpu.CompilerParams(vmem_limit_bytes=vmem * 1024 * 1024),
        cost_estimate=pl.CostEstimate(flops=flops, bytes_accessed=moved, transcendentals=0),
    )


def swap(value, distance, size):
    return lax.ppermute(value, AXES, [(i, i ^ distance) for i in range(size)])


def logical(values, amount):
    return lax.shift_right_logical(values, jnp.full(values.shape, amount, I32))


def contract_last(left, right):
    return lax.dot_general(
        left, right, (((1,), (1,)), ((), ())), preferred_element_type=F32
    )


def columns(me, part, parts, width):
    return pl.ds(pl.multiple_of(((me % parts) ^ part) * width, LANES), width)


def pack(tokens, cotangent, gate_prob, routes, slots):
    group, width = tokens.shape
    top = gate_prob.shape[1]

    def put(value, row, start):
        stop = width + LANES - start - value.shape[1]
        zero = jnp.zeros((), value.dtype)
        return lax.pad(value[None], zero, ((row, 1 - row, 0), (0, 0, 0), (start, stop, 0)))

    def rounded(value):
        return lax.reduce_precision(value, 8, 7)

    high, middle, low = (put(gate_prob, 0, width + i * top) for i in (2, 3, 4))
    rest = low - rounded(low)
    return (
        put(tokens, 0, 0).astype(F32)
        + put(cotangent, 1, 0).astype(F32)
        + put(routes, 0, width).astype(F32)
        + put(slots, 0, width + top).astype(F32)
        + rounded(high)
        + rounded(middle - rounded(middle))
        + (rest - rounded(rest))
    ).astype(BF16)


def load_kernel(count, *refs):
    sems = refs[-1]
    copies = [
        pltpu.make_async_copy(refs[i], refs[count + 1 + i], sems.at[i]) for i in range(count)
    ]
    for copy in copies:
        copy.start()
    for copy in copies:
        copy.wait()


def load(weights, after, vmem):
    count = len(weights)
    return call(
        lambda *refs: load_kernel(count, *refs), [HBM] * count + [VMEM], [VMEM] * count,
        [shape(w.shape) for w in weights], [pltpu.SemaphoreType.DMA((count,))],
        moved=2 * count * weights[0].size, vmem=vmem,
    )(*weights, after)


def plan_kernel(
    bits, parts, top, place_ref, seed_ref, layer_ref, own_ref, other_ref, gate_ref, keep_ref
):
    notes = jnp.concatenate([own_ref[...], other_ref[...]], axis=0).astype(F32)
    rows = notes.shape[0]
    group = rows >> bits
    expert = place_ref[0] // parts
    lane = lax.broadcasted_iota(I32, (rows, LANES), 1)

    def field(i):
        return pltpu.roll(notes, LANES - i * top, 1) if i else notes

    slots = field(1)
    chosen = (
        (lane < top)
        & (field(0) == jnp.full((rows, LANES), expert, I32).astype(F32))
        & (slots < CAP_SRC)
    )
    gate = jnp.where(chosen, field(2) + field(3) + field(4), 0.0)
    gate_ref[...] = jnp.sum(gate, axis=1, keepdims=True)
    slot = jnp.sum(jnp.where(chosen, slots, 0.0), axis=1, keepdims=True).astype(I32)
    position = lax.broadcasted_iota(I32, (rows, 1), 0) // group
    offset = jnp.zeros((rows, 1), I32)
    for b in range(bits):
        offset = offset + (((position >> b) & 1) << (bits - 1 - b))
    row_ids = (expert << bits) * CAP_SRC + (offset ^ expert) * CAP_SRC + slot
    base = row_ids * FF * -1640531535 + seed_ref[0] * 40503 + layer_ref[0] * 97
    units = keep_ref.shape[1]
    unit_ids = (place_ref[0] % parts) * units + lax.broadcasted_iota(I32, (rows, units), 1)
    mixed = base + unit_ids * -1640531535
    mixed = mixed ^ logical(mixed, 15)
    mixed = mixed * -2048144789
    mixed = mixed ^ logical(mixed, 13)
    mixed = mixed * -1028477387
    mixed = mixed ^ logical(mixed, 16)
    levels = logical(mixed, 8) & 1023
    keep_ref[...] = jnp.where(levels >= 102, KEEP_FACTOR, 0.0).astype(F32)


def pre_kernel(part, first, *refs):
    place_ref, own_ref, other_ref, gate_ref, wg, wu, wd = refs[:7]
    x_ref, dy_ref, acc_ref = refs[-3:]
    width = own_ref.shape[2]
    cols = columns(place_ref[0], part, wg.shape[1] // width, width)
    x = jnp.concatenate([own_ref[0], other_ref[0]], axis=0)
    c = jnp.concatenate([own_ref[1], other_ref[1]], axis=0)
    dy = (gate_ref[...] * c.astype(F32)).astype(BF16)
    x_ref[...] = x
    dy_ref[...] = dy
    for i, (left, weight) in enumerate(((x, wg), (x, wu), (dy, wd))):
        term = contract_last(left, weight[:, cols])
        acc_ref[i] = term if first else refs[7][i] + term


def pieces(me, part_ids, g, u, wg, wu, keep_ref, send_ref):
    _, half, width = keep_ref.shape
    for i, part in enumerate(part_ids):
        cols = columns(me, part, wg.shape[1] // width, width)
        piece = (
            jnp.dot(g, wg[:, cols], preferred_element_type=F32)
            + jnp.dot(u, wu[:, cols], preferred_element_type=F32)
        ).astype(BF16)
        keep_ref[i] = piece[:half]
        send_ref[i] = piece[half:]


def hidden_kernel(
    part_ids, place_ref, mul_ref, acc_ref, wg, wu, keep_ref, send_ref, h_ref, g_ref, u_ref
):
    keep_mul = mul_ref[...]
    gate_pre = acc_ref[0]
    up_pre = acc_ref[1]
    grad_hidden = acc_ref[2] * keep_mul
    logistic = jax.nn.sigmoid(gate_pre)
    swish = gate_pre * logistic
    u = (grad_hidden * swish).astype(BF16)
    g = grad_hidden * up_pre * logistic * (1.0 + gate_pre * (1.0 - logistic))
    g = g.astype(BF16)
    h_ref[...] = (swish * up_pre * keep_mul).astype(BF16)
    g_ref[...] = g
    u_ref[...] = u
    pieces(place_ref[0], part_ids, g, u, wg, wu, keep_ref, send_ref)


def piece_kernel(part_ids, place_ref, g_ref, u_ref, wg, wu, keep_ref, send_ref):
    pieces(place_ref[0], part_ids, g_ref[...], u_ref[...], wg, wu, keep_ref, send_ref)


def turning_kernel(
    part_ids, place_ref, h_ref, g_ref, u_ref, wg, wu, keep_ref, send_ref, *turned_refs
):
    piece_kernel(part_ids, place_ref, g_ref, u_ref, wg, wu, keep_ref, send_ref)
    for ref, turned_ref in zip((h_ref, g_ref, u_ref), turned_refs):
        turned_ref[...] = ref[...].astype(F32).T.astype(BF16)


def weight_kernel(jobs, parts, cuts, place_ref, *refs):
    outs, held, sems = refs[-len(jobs) - 2:-2], refs[-2], refs[-1]
    units, width = held.shape[1:]
    copies, n, at = [], 0, 0
    for out, ids in zip(outs, jobs):
        left = refs[at]
        for k, j in enumerate(ids):
            cols = columns(place_ref[0], j, parts, width)
            step = units // (cuts if n == 0 else 1)
            for r in range(0, units, step):
                rows = slice(r, r + step)
                held[n, rows] = jnp.dot(
                    left[rows], refs[at + 1 + k][...], preferred_element_type=F32
                ).astype(BF16)
                copies.append(
                    pltpu.make_async_copy(
                        held.at[n, rows], out.at[rows, cols], sems.at[len(copies)]
                    )
                )
                copies[-1].start()
            n += 1
        at += 1 + len(ids)
    for copy in copies:
        copy.wait()


def weight_grads(place, jobs):
    parts = len(jobs[0][1])
    rows, width = jobs[0][1][0].shape
    units = jobs[0][0].shape[0]
    cuts = 4 if units % 64 == 0 else 1
    ids = [job[2] for job in jobs]
    count = sum(len(i) for i in ids)
    flat = [x for left, right, i, _ in jobs for x in [left] + [right[j] for j in i]]
    begun = [job[3] for job in jobs if job[3] is not None]
    aliases, at = {}, 1 + len(flat)
    for n, job in enumerate(jobs):
        if job[3] is not None:
            aliases[at] = n
            at += 1
    return pl.pallas_call(
        lambda *refs: weight_kernel(ids, parts, cuts, *refs),
        in_specs=[SMEM] + [VMEM] * len(flat) + [HBM] * len(begun),
        out_specs=[HBM] * len(jobs),
        out_shape=[shape((units, parts * width))] * len(jobs),
        scratch_shapes=[
            pltpu.VMEM((count, units, width), BF16), pltpu.SemaphoreType.DMA((count + cuts - 1,))
        ],
        input_output_aliases=aliases,
        compiler_params=pltpu.CompilerParams(vmem_limit_bytes=20 * 1024 * 1024),
        cost_estimate=pl.CostEstimate(
            flops=2 * count * units * rows * width,
            bytes_accessed=2 * count * units * width,
            transcendentals=0,
        ),
    )(place, *flat, *begun)


def add(kept, *came):
    total = kept.astype(F32)
    for block in came:
        total = total + block.astype(F32)
    return total.astype(BF16)


def token_device(
    tokens, cotangent, gate_prob, routes, slots, drop_seed, layer_id, w_gate, w_up, w_down
):
    experts = lax.axis_size("expert")
    parts = lax.axis_size("hid")
    size = experts * parts
    group, width = tokens.shape
    top = gate_prob.shape[1]
    units = w_gate.shape[1]
    rows = experts * group
    half = rows // 2
    bits = experts.bit_length() - 1
    place = lax.axis_index(AXES).astype(I32)[None]
    wg, wu, wd = w_gate[0], w_up[0], w_down[0]
    data = pack(tokens, cotangent, gate_prob, routes, slots)
    data, place = lax.optimization_barrier((data, place))
    distance = experts // 2
    loads, loaded = [([wg], 48), ([wu, wd], 40)], []
    while distance > 1:
        came = swap(data, distance * parts, size)
        if loads:
            held = load(loads[0][0], data, loads[0][1])
            came, *held = lax.optimization_barrier((came, *held))
            loads, loaded = loads[1:], loaded + held
        data = jnp.concatenate([data, came], axis=1)
        distance //= 2
    wg, wu, wd = loaded + [w for pair in loads for w in pair[0]]
    notes = data[0, :, width:]
    own = [data[:, :, :width]]
    own += [swap(own[0], j, size) for j in range(1, parts)]
    other_notes = swap(notes, parts, size)
    gate, keep_mul = call(
        lambda *refs: plan_kernel(bits, parts, top, *refs),
        [SMEM] * 3 + [VMEM] * 2, [VMEM] * 2,
        [shape((rows, 1), F32), shape((rows, units), F32)],
    )(place, drop_seed, layer_id, notes, other_notes)
    xs, dys, acc = [None] * parts, [None] * parts, None
    order = [0] + list(range(1, parts))[::-1]
    order = order[:2] + order[2:][::-1]
    others = [swap(own[0], parts, size)] + [None] * (parts - 1)
    for n, j in enumerate(order):
        held = [] if acc is None else [acc]
        other = others[j]
        xs[j], dys[j], acc = call(
            lambda *refs, j=j, n=n: pre_kernel(j, n == 0, *refs),
            [SMEM] + [VMEM] * (6 + len(held)), [VMEM] * 3,
            [shape((rows, width)), shape((rows, width)), shape((3, rows, units), F32)],
            flops=6 * rows * units * width, moved=6 * units * width,
        )(place, own[j], other, gate, wg, wu, wd, *held)
        if n == 0:
            came = lax.optimization_barrier((acc, own[order[1]]))
            acc, own[order[1]] = came
            others[order[1]] = swap(own[order[1]], parts, size)
        if n + 2 < parts:
            i, k = order[n + 1], order[n + 2]
            others[k] = swap(own[k], parts, size)
            others[i], others[k] = others[i], others[k]
    high, low, mine = [parts - 1], list(range(1, parts - 1)), [0]
    block, blocks = (shape((len(ids), half, width)) for ids in (high, low))
    turned = shape((units, rows))
    straight = shape((rows, units))
    flops = 4 * rows * units * width * (parts // 2)
    keep, send, h, g, u = call(
        lambda *refs: hidden_kernel(high, *refs), [SMEM] + [VMEM] * 4, [VMEM] * 5,
        [block, block, straight, straight, straight],
        flops=flops, moved=2 * units * width * parts,
    )(place, keep_mul, acc, wg, wu)
    upper_keep, upper_came = keep, swap(send, parts, size)
    keep, send, hid_t, g_t, u_t = call(
        lambda *refs: turning_kernel(low, *refs), [SMEM] + [VMEM] * 5, [VMEM] * 5,
        [blocks, blocks, turned, turned, turned], flops=flops, moved=2 * units * width * parts,
    )(place, h, g, u, wg, wu)
    upper_came, keep, send = lax.optimization_barrier((upper_came, keep, send))
    upper = add(upper_keep, upper_came)
    lower = add(keep, swap(send, parts, size))
    later_g = lax.optimization_barrier((g, lower))[0]
    keep, send = call(
        lambda *refs: piece_kernel(mine, *refs), [SMEM] + [VMEM] * 4, [VMEM] * 2,
        [block, block], flops=flops, moved=2 * units * width * parts,
    )(place, later_g, u, wg, wu)
    own = add(keep, swap(send, parts, size))
    every, front, back = list(range(parts)), list(range(parts // 2)), list(range(parts // 2, parts))

    def rounds(kept, sends, after, jobs):
        came = [swap(block, distance, size) for block, distance in sends]
        made = []
        if jobs:
            lefts = lax.optimization_barrier((tuple(job[0] for job in jobs), after))[0]
            made = weight_grads(place, [(left, *job[1:]) for left, job in zip(lefts, jobs)])
            *came, made = lax.optimization_barrier((*came, made))
        return add(kept, *came), made

    sends = [(upper[0], high[0])] + [(lower[i], low[i]) for i in range(len(low))][::-1]
    waiting, _ = lax.optimization_barrier((tuple(block for block, _ in sends[1:]), lower))
    sends[1:] = [(block, send[1]) for block, send in zip(waiting, sends[1:])]
    part, (grad_down, grad_gate) = rounds(
        own[0], sends, lower, [(hid_t, dys, every, None), (g_t, xs, front, None)]
    )
    part = part.reshape(experts // 2, group, width)
    distance, grad_up = experts // 2, None
    while distance > 1:
        kept, away = part[0::2], part[1::2]
        jobs = []
        if distance == experts // 2:
            jobs = [(g_t, xs, back, grad_gate), (u_t, xs, every[:1], None)]
        elif distance == experts // 4:
            jobs = [(u_t, xs, every[1:], grad_up)]
        part, made = rounds(kept, [(away, distance * parts)], away, jobs)
        if distance == experts // 2:
            grad_gate, grad_up = made
        elif jobs:
            (grad_up,) = made
        distance //= 2
    if experts == 2:
        (grad_gate,) = weight_grads(place, [(g_t, xs, back, grad_gate)])
        (grad_up,) = weight_grads(place, [(u_t, xs, every, None)])
    elif experts == 4:
        (grad_up,) = weight_grads(place, [(u_t, xs, every[1:], grad_up)])
    return (part[0], grad_gate[None], grad_up[None], grad_down[None])


def power_of_two(number):
    return number & (number - 1) == 0


def on_device(*args):
    tokens, gate_prob, w_gate = args[0], args[2], args[7]
    experts = lax.axis_size("expert")
    parts = lax.axis_size("hid")
    few = tokens.shape[0] <= CAP_SRC and experts <= 256
    noted = 5 * gate_prob.shape[1] <= LANES
    even = power_of_two(experts) and power_of_two(parts) and experts > 1 and parts > 1
    tiled = (
        tokens.shape[0] % 8 == 0
        and tokens.shape[1] % LANES == 0
        and w_gate.shape[1] % LANES == 0
    )
    if few and noted and even and tiled:
        return token_device(*args)
    return general_device(*args)


def solution(mesh):
    in_specs = (
        P("expert", "hid"),
        P("expert", "hid"),
        P("expert", None),
        P("expert", None),
        P("expert", None),
        P(),
        P(),
        P("expert", "hid", None),
        P("expert", "hid", None),
        P("expert", "hid", None),
    )
    out_specs = (
        P("expert", "hid"),
        P("expert", "hid", None),
        P("expert", "hid", None),
        P("expert", "hid", None),
    )
    return jax.shard_map(
        on_device, mesh=mesh, in_specs=in_specs, out_specs=out_specs, check_vma=False
    )
```

```python
import jax
import jax.numpy as jnp
from jax import lax
from jax.experimental import pallas as pl
from jax.experimental.pallas import tpu as pltpu
from jax.sharding import PartitionSpec as P

FF = 2560
CAP_SRC = 8


KEEP_FACTOR = 1024.0 / 922.0


def logical_shift(values, amount):
    return jnp.right_shift(values, amount) & (1 << 32 - amount) - 1


def keep_mask(counter, seed_value, layer_value):
    mixed = counter * -1640531535 + seed_value * 40503 + layer_value * 97
    mixed = mixed ^ logical_shift(mixed, 15)
    mixed = mixed * -2048144789
    mixed = mixed ^ logical_shift(mixed, 13)
    mixed = mixed * -1028477387
    mixed = mixed ^ logical_shift(mixed, 16)
    levels = logical_shift(mixed, 8) & 1023
    return jnp.where(levels >= 102, KEEP_FACTOR, 0.0).astype(jnp.float32)


def contract_rows(left, right):
    return lax.dot_general(
        left, right, (((0,), (0,)), ((), ())), preferred_element_type=jnp.float32
    )


def contract_cols(left, right):
    return lax.dot_general(
        left, right, (((1,), (1,)), ((), ())), preferred_element_type=jnp.float32
    )


def general_device(
    tokens, cotangent, gate_prob, routes, slots, drop_seed, layer_id, w_gate, w_up, w_down
):
    experts = lax.axis_size("expert")
    part_width = tokens.shape[1]
    capacity = experts * CAP_SRC
    local_units = w_gate.shape[1]
    target = jnp.where(slots < CAP_SRC, routes * CAP_SRC + slots, -1)
    slot_ids = jnp.arange(experts * CAP_SRC, dtype=jnp.int32)
    matches = target[None, :, :] == slot_ids[:, None, None]
    placed = jnp.any(matches, axis=2).astype(jnp.bfloat16)
    slot_gate = jnp.sum(jnp.where(matches, gate_prob[None, :, :], 0.0), axis=(1, 2))
    sent_x = jnp.dot(placed, tokens, preferred_element_type=jnp.float32).astype(jnp.bfloat16)
    plain_dy = jnp.dot(placed, cotangent, preferred_element_type=jnp.float32)
    sent_dy = (slot_gate[:, None] * plain_dy).astype(jnp.bfloat16)
    send_shape = (experts, CAP_SRC * part_width)
    recv_x, recv_dy = (
        lax.all_to_all(
            sent_x.reshape(send_shape), "expert", split_axis=0, concat_axis=0, tiled=True
        ),
        lax.all_to_all(
            sent_dy.reshape(send_shape), "expert", split_axis=0, concat_axis=0, tiled=True
        ),
    )
    rows_x, rows_dy = (
        lax.all_gather(recv_x.reshape(capacity, part_width), "hid", axis=1, tiled=True),
        lax.all_gather(recv_dy.reshape(capacity, part_width), "hid", axis=1, tiled=True),
    )
    gate_w = w_gate[0]
    up_w = w_up[0]
    down_w = w_down[0]
    gate_pre = contract_cols(rows_x, gate_w)
    up_pre = contract_cols(rows_x, up_w)
    expert_id = lax.axis_index("expert")
    unit_ids = lax.axis_index("hid") * local_units + jnp.arange(local_units, dtype=jnp.int32)
    row_ids = jnp.arange(capacity, dtype=jnp.int32)
    counter = (expert_id * capacity + row_ids[:, None]) * FF + unit_ids[None, :]
    keep_mul = keep_mask(counter, drop_seed[0], layer_id[0])
    logistic = jax.nn.sigmoid(gate_pre)
    swish = gate_pre * logistic
    hidden = (swish * up_pre * keep_mul).astype(jnp.bfloat16)
    grad_hidden = contract_cols(rows_dy, down_w) * keep_mul
    grad_upre = (grad_hidden * swish).astype(jnp.bfloat16)
    grad_gpre = (grad_hidden * up_pre * logistic * (1.0 + gate_pre * (1.0 - logistic))).astype(
        jnp.bfloat16
    )
    grad_down = contract_rows(hidden, rows_dy).astype(jnp.bfloat16)
    grad_gate = contract_rows(grad_gpre, rows_x).astype(jnp.bfloat16)
    grad_up = contract_rows(grad_upre, rows_x).astype(jnp.bfloat16)
    partial_sum = jnp.dot(grad_gpre, gate_w, preferred_element_type=jnp.float32) + jnp.dot(
        grad_upre, up_w, preferred_element_type=jnp.float32
    )
    summed = lax.psum(partial_sum.astype(jnp.bfloat16), "hid").astype(jnp.float32)
    own_cols = lax.dynamic_slice_in_dim(summed, lax.axis_index("hid") * part_width, part_width, 1)
    back_rows = lax.all_to_all(
        own_cols.astype(jnp.bfloat16).reshape(send_shape),
        "expert",
        split_axis=0,
        concat_axis=0,
        tiled=True,
    )
    grad_tokens = contract_rows(placed, back_rows.reshape(experts * CAP_SRC, part_width)).astype(
        jnp.bfloat16
    )
    return (grad_tokens, grad_gate[None], grad_up[None], grad_down[None])


BF16 = jnp.bfloat16
F32 = jnp.float32
I32 = jnp.int32
AXES = ("expert", "hid")
LANES = 128
HBM = pl.BlockSpec(memory_space=pltpu.HBM)
VMEM = pl.BlockSpec(memory_space=pltpu.VMEM)
SMEM = pl.BlockSpec(memory_space=pltpu.SMEM)


def shape(dims, dtype=BF16):
    return jax.ShapeDtypeStruct(dims, dtype)


def call(kernel, ins, outs, out_shape, scratch=(), flops=0, moved=0, vmem=8):
    return pl.pallas_call(
        kernel,
        in_specs=ins,
        out_specs=outs,
        out_shape=out_shape,
        scratch_shapes=list(scratch),
        compiler_params=pltpu.CompilerParams(vmem_limit_bytes=vmem * 1024 * 1024),
        cost_estimate=pl.CostEstimate(flops=flops, bytes_accessed=moved, transcendentals=0),
    )


def swap(value, distance, size):
    return lax.ppermute(value, AXES, [(i, i ^ distance) for i in range(size)])


def logical(values, amount):
    return lax.shift_right_logical(values, jnp.full(values.shape, amount, I32))


def contract_last(left, right):
    return lax.dot_general(
        left, right, (((1,), (1,)), ((), ())), preferred_element_type=F32
    )


def columns(me, part, parts, width):
    return pl.ds(pl.multiple_of(((me % parts) ^ part) * width, LANES), width)


def pack(tokens, cotangent, gate_prob, routes, slots):
    group, width = tokens.shape
    top = gate_prob.shape[1]

    def put(value, row, start):
        stop = width + LANES - start - value.shape[1]
        zero = jnp.zeros((), value.dtype)
        return lax.pad(value[None], zero, ((row, 1 - row, 0), (0, 0, 0), (start, stop, 0)))

    def rounded(value):
        return lax.reduce_precision(value, 8, 7)

    high, middle, low = (put(gate_prob, 0, width + i * top) for i in (2, 3, 4))
    rest = low - rounded(low)
    return (
        put(tokens, 0, 0).astype(F32)
        + put(cotangent, 1, 0).astype(F32)
        + put(routes, 0, width).astype(F32)
        + put(slots, 0, width + top).astype(F32)
        + rounded(high)
        + rounded(middle - rounded(middle))
        + (rest - rounded(rest))
    ).astype(BF16)


def load_kernel(count, *refs):
    sems = refs[-1]
    copies = [
        pltpu.make_async_copy(refs[i], refs[count + 1 + i], sems.at[i]) for i in range(count)
    ]
    for copy in copies:
        copy.start()
    for copy in copies:
        copy.wait()


def load(weights, after, vmem):
    count = len(weights)
    return call(
        lambda *refs: load_kernel(count, *refs), [HBM] * count + [VMEM], [VMEM] * count,
        [shape(w.shape) for w in weights], [pltpu.SemaphoreType.DMA((count,))],
        moved=2 * count * weights[0].size, vmem=vmem,
    )(*weights, after)


def plan_kernel(
    bits, parts, top, place_ref, seed_ref, layer_ref, own_ref, other_ref, gate_ref, keep_ref
):
    notes = jnp.concatenate([own_ref[...], other_ref[...]], axis=0).astype(F32)
    rows = notes.shape[0]
    group = rows >> bits
    expert = place_ref[0] // parts
    lane = lax.broadcasted_iota(I32, (rows, LANES), 1)

    def field(i):
        return pltpu.roll(notes, LANES - i * top, 1) if i else notes

    slots = field(1)
    chosen = (
        (lane < top)
        & (field(0) == jnp.full((rows, LANES), expert, I32).astype(F32))
        & (slots < CAP_SRC)
    )
    gate = jnp.where(chosen, field(2) + field(3) + field(4), 0.0)
    gate_ref[...] = jnp.sum(gate, axis=1, keepdims=True)
    slot = jnp.sum(jnp.where(chosen, slots, 0.0), axis=1, keepdims=True).astype(I32)
    position = lax.broadcasted_iota(I32, (rows, 1), 0) // group
    offset = jnp.zeros((rows, 1), I32)
    for b in range(bits):
        offset = offset + (((position >> b) & 1) << (bits - 1 - b))
    row_ids = (expert << bits) * CAP_SRC + (offset ^ expert) * CAP_SRC + slot
    base = row_ids * FF * -1640531535 + seed_ref[0] * 40503 + layer_ref[0] * 97
    units = keep_ref.shape[1]
    unit_ids = (place_ref[0] % parts) * units + lax.broadcasted_iota(I32, (rows, units), 1)
    mixed = base + unit_ids * -1640531535
    mixed = mixed ^ logical(mixed, 15)
    mixed = mixed * -2048144789
    mixed = mixed ^ logical(mixed, 13)
    mixed = mixed * -1028477387
    mixed = mixed ^ logical(mixed, 16)
    levels = logical(mixed, 8) & 1023
    keep_ref[...] = jnp.where(levels >= 102, KEEP_FACTOR, 0.0).astype(F32)


def products(part, place_ref, own_ref, other_ref, gate_ref, wg, wu, wd, x_ref, dy_ref, acc_ref):
    width = own_ref.shape[2]
    cols = columns(place_ref[0], part, wg.shape[1] // width, width)
    x = jnp.concatenate([own_ref[0], other_ref[0]], axis=0)
    c = jnp.concatenate([own_ref[1], other_ref[1]], axis=0)
    dy = (gate_ref[...] * c.astype(F32)).astype(BF16)
    x_ref[...] = x
    dy_ref[...] = dy
    terms = [contract_last(left, w[:, cols]) for left, w in ((x, wg), (x, wu), (dy, wd))]
    return terms if acc_ref is None else [acc_ref[i] + term for i, term in enumerate(terms)]


def pre_kernel(part, first, *refs):
    x_ref, dy_ref, acc_ref = refs[-3:]
    before = None if first else refs[7]
    for i, term in enumerate(products(part, *refs[:7], x_ref, dy_ref, before)):
        acc_ref[i] = term


def pieces(me, part_ids, g, u, wg, wu, keep_ref, send_ref):
    _, half, width = keep_ref.shape
    for i, part in enumerate(part_ids):
        cols = columns(me, part, wg.shape[1] // width, width)
        piece = (
            jnp.dot(g, wg[:, cols], preferred_element_type=F32)
            + jnp.dot(u, wu[:, cols], preferred_element_type=F32)
        ).astype(BF16)
        keep_ref[i] = piece[:half]
        send_ref[i] = piece[half:]


def hidden_kernel(
    part, part_ids, place_ref, own_ref, other_ref, gate_ref, wg, wu, wd, acc_ref, mul_ref,
    x_ref, dy_ref, keep_ref, send_ref, h_ref, g_ref, u_ref,
):
    keep_mul = mul_ref[...]
    gate_pre, up_pre, grad_hidden = products(
        part, place_ref, own_ref, other_ref, gate_ref, wg, wu, wd, x_ref, dy_ref, acc_ref
    )
    grad_hidden = grad_hidden * keep_mul
    logistic = jax.nn.sigmoid(gate_pre)
    swish = gate_pre * logistic
    u = (grad_hidden * swish).astype(BF16)
    g = grad_hidden * up_pre * logistic * (1.0 + gate_pre * (1.0 - logistic))
    g = g.astype(BF16)
    h_ref[...] = (swish * up_pre * keep_mul).astype(BF16)
    g_ref[...] = g
    u_ref[...] = u
    pieces(place_ref[0], part_ids, g, u, wg, wu, keep_ref, send_ref)


def piece_kernel(part_ids, place_ref, g_ref, u_ref, wg, wu, keep_ref, send_ref):
    pieces(place_ref[0], part_ids, g_ref[...], u_ref[...], wg, wu, keep_ref, send_ref)


def turning_kernel(
    part_ids, place_ref, h_ref, g_ref, u_ref, wg, wu, keep_ref, send_ref, *turned_refs
):
    piece_kernel(part_ids, place_ref, g_ref, u_ref, wg, wu, keep_ref, send_ref)
    for ref, turned_ref in zip((h_ref, g_ref, u_ref), turned_refs):
        turned_ref[...] = ref[...].astype(F32).T.astype(BF16)


def weight_kernel(jobs, parts, cuts, place_ref, *refs):
    outs, held, sems = refs[-len(jobs) - 2:-2], refs[-2], refs[-1]
    units, width = held.shape[1:]
    copies, n, at = [], 0, 0
    for out, ids in zip(outs, jobs):
        left = refs[at]
        for k, j in enumerate(ids):
            cols = columns(place_ref[0], j, parts, width)
            step = units // (cuts if n == 0 else 1)
            for r in range(0, units, step):
                rows = slice(r, r + step)
                held[n, rows] = jnp.dot(
                    left[rows], refs[at + 1 + k][...], preferred_element_type=F32
                ).astype(BF16)
                copies.append(
                    pltpu.make_async_copy(
                        held.at[n, rows], out.at[rows, cols], sems.at[len(copies)]
                    )
                )
                copies[-1].start()
            n += 1
        at += 1 + len(ids)
    for copy in copies:
        copy.wait()


def weight_grads(place, jobs):
    parts = len(jobs[0][1])
    rows, width = jobs[0][1][0].shape
    units = jobs[0][0].shape[0]
    cuts = 4 if units % 64 == 0 else 1
    ids = [job[2] for job in jobs]
    count = sum(len(i) for i in ids)
    flat = [x for left, right, i, _ in jobs for x in [left] + [right[j] for j in i]]
    begun = [job[3] for job in jobs if job[3] is not None]
    aliases, at = {}, 1 + len(flat)
    for n, job in enumerate(jobs):
        if job[3] is not None:
            aliases[at] = n
            at += 1
    return pl.pallas_call(
        lambda *refs: weight_kernel(ids, parts, cuts, *refs),
        in_specs=[SMEM] + [VMEM] * len(flat) + [HBM] * len(begun),
        out_specs=[HBM] * len(jobs),
        out_shape=[shape((units, parts * width))] * len(jobs),
        scratch_shapes=[
            pltpu.VMEM((count, units, width), BF16), pltpu.SemaphoreType.DMA((count + cuts - 1,))
        ],
        input_output_aliases=aliases,
        compiler_params=pltpu.CompilerParams(vmem_limit_bytes=20 * 1024 * 1024),
        cost_estimate=pl.CostEstimate(
            flops=2 * count * units * rows * width,
            bytes_accessed=2 * count * units * width,
            transcendentals=0,
        ),
    )(place, *flat, *begun)


def add(kept, *came):
    total = kept.astype(F32)
    for block in came:
        total = total + block.astype(F32)
    return total.astype(BF16)


def token_device(
    tokens, cotangent, gate_prob, routes, slots, drop_seed, layer_id, w_gate, w_up, w_down
):
    experts = lax.axis_size("expert")
    parts = lax.axis_size("hid")
    size = experts * parts
    group, width = tokens.shape
    top = gate_prob.shape[1]
    units = w_gate.shape[1]
    rows = experts * group
    half = rows // 2
    bits = experts.bit_length() - 1
    place = lax.axis_index(AXES).astype(I32)[None]
    wg, wu, wd = w_gate[0], w_up[0], w_down[0]
    data = pack(tokens, cotangent, gate_prob, routes, slots)
    data, place = lax.optimization_barrier((data, place))
    distance = experts // 2
    loads, loaded = [([wg], 48), ([wu, wd], 40)], []
    while distance > 1:
        came = swap(data, distance * parts, size)
        if loads:
            held = load(loads[0][0], data, loads[0][1])
            came, *held = lax.optimization_barrier((came, *held))
            loads, loaded = loads[1:], loaded + held
        data = jnp.concatenate([data, came], axis=1)
        distance //= 2
    wg, wu, wd = loaded + [w for pair in loads for w in pair[0]]
    notes = data[0, :, width:]
    own = [data[:, :, :width]]
    own += [swap(own[0], j, size) for j in range(1, parts)]
    other_notes = swap(notes, parts, size)
    gate, keep_mul = call(
        lambda *refs: plan_kernel(bits, parts, top, *refs),
        [SMEM] * 3 + [VMEM] * 2, [VMEM] * 2,
        [shape((rows, 1), F32), shape((rows, units), F32)],
    )(place, drop_seed, layer_id, notes, other_notes)
    xs, dys, acc = [None] * parts, [None] * parts, None
    order = [0] + list(range(1, parts))[::-1]
    order = order[:2] + order[2:][::-1]
    others = [swap(own[0], parts, size)] + [None] * (parts - 1)
    for n, j in enumerate(order):
        held = [] if acc is None else [acc]
        other = others[j]
        if n == parts - 1:
            break
        xs[j], dys[j], acc = call(
            lambda *refs, j=j, n=n: pre_kernel(j, n == 0, *refs),
            [SMEM] + [VMEM] * (6 + len(held)), [VMEM] * 3,
            [shape((rows, width)), shape((rows, width)), shape((3, rows, units), F32)],
            flops=6 * rows * units * width, moved=6 * units * width,
        )(place, own[j], other, gate, wg, wu, wd, *held)
        if n == 0:
            came = lax.optimization_barrier((acc, own[order[1]]))
            acc, own[order[1]] = came
            others[order[1]] = swap(own[order[1]], parts, size)
        if n + 2 < parts:
            i, k = order[n + 1], order[n + 2]
            others[k] = swap(own[k], parts, size)
            others[i], others[k] = others[i], others[k]
    high, low, mine = [parts - 1], list(range(1, parts - 1)), [0]
    block, blocks = (shape((len(ids), half, width)) for ids in (high, low))
    turned = shape((units, rows))
    straight = shape((rows, units))
    flops = 4 * rows * units * width * (parts // 2)
    last = order[-1]
    xs[last], dys[last], keep, send, h, g, u = call(
        lambda *refs: hidden_kernel(last, high, *refs), [SMEM] + [VMEM] * 8, [VMEM] * 7,
        [shape((rows, width)), shape((rows, width)), block, block, straight, straight, straight],
        flops=flops, moved=2 * units * width * parts,
    )(place, own[last], others[last], gate, wg, wu, wd, acc, keep_mul)
    upper_keep, upper_came = keep, swap(send, parts, size)
    keep, send, hid_t, g_t, u_t = call(
        lambda *refs: turning_kernel(low, *refs), [SMEM] + [VMEM] * 5, [VMEM] * 5,
        [blocks, blocks, turned, turned, turned], flops=flops, moved=2 * units * width * parts,
    )(place, h, g, u, wg, wu)
    upper_came, keep, send = lax.optimization_barrier((upper_came, keep, send))
    upper = add(upper_keep, upper_came)
    lower = add(keep, swap(send, parts, size))
    later_g = lax.optimization_barrier((g, lower))[0]
    keep, send = call(
        lambda *refs: piece_kernel(mine, *refs), [SMEM] + [VMEM] * 4, [VMEM] * 2,
        [block, block], flops=flops, moved=2 * units * width * parts,
    )(place, later_g, u, wg, wu)
    own = add(keep, swap(send, parts, size))
    every, front, back = list(range(parts)), list(range(parts // 2)), list(range(parts // 2, parts))

    def rounds(kept, sends, after, jobs):
        came = [swap(block, distance, size) for block, distance in sends]
        made = []
        if jobs:
            lefts = lax.optimization_barrier((tuple(job[0] for job in jobs), after))[0]
            made = weight_grads(place, [(left, *job[1:]) for left, job in zip(lefts, jobs)])
            *came, made = lax.optimization_barrier((*came, made))
        return add(kept, *came), made

    sends = [(upper[0], high[0])] + [(lower[i], low[i]) for i in range(len(low))][::-1]
    waiting, _ = lax.optimization_barrier((tuple(block for block, _ in sends[1:]), lower))
    sends[1:] = [(block, send[1]) for block, send in zip(waiting, sends[1:])]
    part, (grad_down, grad_gate) = rounds(
        own[0], sends, lower, [(hid_t, dys, every, None), (g_t, xs, front, None)]
    )
    part = part.reshape(experts // 2, group, width)
    distance, grad_up = experts // 2, None
    while distance > 1:
        kept, away = part[0::2], part[1::2]
        jobs = []
        if distance == experts // 2:
            jobs = [(g_t, xs, back, grad_gate), (u_t, xs, every[:1], None)]
        elif distance == experts // 4:
            jobs = [(u_t, xs, every[1:], grad_up)]
        part, made = rounds(kept, [(away, distance * parts)], away, jobs)
        if distance == experts // 2:
            grad_gate, grad_up = made
        elif jobs:
            (grad_up,) = made
        distance //= 2
    if experts == 2:
        (grad_gate,) = weight_grads(place, [(g_t, xs, back, grad_gate)])
        (grad_up,) = weight_grads(place, [(u_t, xs, every, None)])
    elif experts == 4:
        (grad_up,) = weight_grads(place, [(u_t, xs, every[1:], grad_up)])
    return (part[0], grad_gate[None], grad_up[None], grad_down[None])


def power_of_two(number):
    return number & (number - 1) == 0


def on_device(*args):
    tokens, gate_prob, w_gate = args[0], args[2], args[7]
    experts = lax.axis_size("expert")
    parts = lax.axis_size("hid")
    few = tokens.shape[0] <= CAP_SRC and experts <= 256
    noted = 5 * gate_prob.shape[1] <= LANES
    even = power_of_two(experts) and power_of_two(parts) and experts > 1 and parts > 1
    tiled = (
        tokens.shape[0] % 8 == 0
        and tokens.shape[1] % LANES == 0
        and w_gate.shape[1] % LANES == 0
    )
    if few and noted and even and tiled:
        return token_device(*args)
    return general_device(*args)


def solution(mesh):
    in_specs = (
        P("expert", "hid"),
        P("expert", "hid"),
        P("expert", None),
        P("expert", None),
        P("expert", None),
        P(),
        P(),
        P("expert", "hid", None),
        P("expert", "hid", None),
        P("expert", "hid", None),
    )
    out_specs = (
        P("expert", "hid"),
        P("expert", "hid", None),
        P("expert", "hid", None),
        P("expert", "hid", None),
    )
    return jax.shard_map(
        on_device, mesh=mesh, in_specs=in_specs, out_specs=out_specs, check_vma=False
    )
```
